256 devices in a mesh: dp: 4 (over z_lo), expert: 64 (over x, y, z_hi, core).
Axes of the slice: x: 4, y: 4, z: 8 (z_hi: 2, z_lo: 4; z = z_hi * 4 + z_lo), core: 2. Of those that a mesh axis runs over, the one named last changes fastest.
Arguments:
- tokens: bfloat16 [2, 4096, 4096], P(None, ('dp', 'expert')), may hold values from -6 to 6
- expert_ids: int32 [2, 4096, 8], P(None, ('dp', 'expert')), may hold values from 0 to 63, all different within a row; in each aligned block of 16 rows (0 to 15, 16 to 31, ..., all dimensions but the last counted through in order) at most 3 rows name the same one
- gate_probs: float32 [2, 4096, 8], P(None, ('dp', 'expert')), may hold values from 0.1 to 1
- gate_up: bfloat16 [64, 2, 768, 4096], P('expert', None, 'dp'), may hold values from -0.09375 to 0.09375
- down_proj: bfloat16 [64, 768, 4096], P('expert', 'dp'), may hold values from -0.21875 to 0.21875
- pairs: int32 [8, 2], replicated, may hold values from 0 to 63, as said below
Outputs:
- moe_out: bfloat16 [2, 4096, 4096], P(None, ('dp', 'expert'))
- placed_gate_up: bfloat16 [64, 2, 768, 4096], P('expert', None, 'dp')
- placed_down: bfloat16 [64, 768, 4096], P('expert', 'dp')
The draws below stay inside these ranges and needn't reach their ends.
Inputs may be any that keep to these rules, and one draw needn't show every extreme that they name: `expert_ids`: in each step, the 16 rows of one device name one expert at most 3 times. `pairs`: each row is (j, j + 32) with j below 32; no slot stands in two rows.
All inputs are finite; a program needn't handle non-finite values.
Results may differ from the reference program's by a relative error of at most 0.012.
Values may be sent and summed in bfloat16 or wider, within the bound.
No kernel may reach another device: no remote copies, remote signals or barrier semaphores. Data moves between devices by JAX's collectives and lax.ppermute only.
A program may use at most 128 MiB of HBM per device.

```python
import math
import jax
import jax.numpy as jnp
import numpy as np
from jax import lax

D = 4096
FF = 768
TOP = 8
STEPS = 2
ROWS_DEV = 16
EXPERTS = 64
TOKENS = 4096
CAP = 3
HALF = 32
PAIRS = 8
N_DP = 4


def draw_pairs(key, part):
    middle = jax.random.permutation(key, jnp.arange(1, HALF - 1, dtype=jnp.int32))
    lower_dev = jnp.concatenate([jnp.array([0, HALF - 1], jnp.int32), middle[:PAIRS - 2]])
    order_key = jax.random.fold_in(key, 7)
    lower_dev = lower_dev[jax.random.permutation(order_key, PAIRS)]
    return jnp.stack([lower_dev, lower_dev + HALF], axis=1).astype(jnp.int32)


def steps_of(stream_key, extent, split, low, high):
    level = 1.0
    for position, shards_of in split:
        steps = jax.random.uniform(jax.random.fold_in(jax.random.fold_in(stream_key, 6), position), (shards_of,), jnp.float32, low / len(split), high / len(split))
        level = level * jnp.repeat(jnp.exp(steps), extent[position] // shards_of).reshape((-1,) + (1,) * (len(extent) - 1 - position))
    return level


def routed_block(rng, own, number, rows, number_of, top, reach, lean):
    ranking = jax.random.permutation(rng, number_of)
    crowded, usual = shares(number_of, rows * top, reach, lean, True), shares(number_of, rows * top, reach, lean, False)
    places = jnp.arange(number_of)

    def named(tallies, offset_by):
        used = int((tallies > 0).sum())
        fixed = max(1, used // 4)
        shifted = fixed + (places - fixed + offset_by * (used - fixed)) % max(1, number_of - fixed)
        return jnp.zeros((number_of,), jnp.int32).at[ranking[jnp.where(places < fixed, places, shifted)]].set(jnp.asarray(tallies, jnp.int32))

    tallies = jnp.where(number % 4 == 0, named(crowded, number // 4), named(usual, number - number // 4 - 1))
    mixed = jax.random.permutation(jax.random.fold_in(own, 3), number_of)
    giver, taker = mixed[0:number_of // 2 * 2:2], mixed[1:number_of // 2 * 2:2]
    margin = jnp.minimum(tallies[giver] - 1, reach - tallies[taker]) // 2
    margin = jnp.where((giver == ranking[0]) | (taker == ranking[0]) | (tallies[taker] == 0), 0, jnp.maximum(margin, 0))
    shifted = jax.random.randint(jax.random.fold_in(own, 4), (number_of // 2,), 0, 1 << 20) % (margin + 1)
    tallies = tallies.at[giver].add(-shifted).at[taker].add(shifted)
    items = jnp.searchsorted(jnp.cumsum(tallies), jnp.arange(rows * top), side="right").astype(jnp.int32)
    table = items.reshape(top, rows).T
    table = table[jax.random.permutation(jax.random.fold_in(own, 1), rows)]
    offset_by = jax.random.randint(jax.random.fold_in(own, 2), (rows, 1), 0, top)
    return jnp.take_along_axis(table, (jnp.arange(top)[None, :] + offset_by) % top, axis=1)


def shares(number_of, total, reach, lean, full):
    portions = [(1 << 20) // math.isqrt(rank ** lean) + 1 for rank in range(1, number_of + 1)]
    largest = reach if full else min(reach, max(-(-total // number_of), total * portions[0] // sum(portions)))
    least = 1 if total - largest >= number_of - 1 else 0
    counts, surplus = [largest] + [least] * (number_of - 1), total - largest - least * (number_of - 1)
    while surplus > 0:
        free = [i for i in range(1, number_of) if counts[i] < largest] or [i for i in range(1, number_of) if counts[i] < reach]
        pool, remaining = sum([portions[i] for i in free]), surplus
        for i in free:
            more = min(reach - counts[i], max(1, remaining * portions[i] // pool), surplus)
            counts[i] = counts[i] + more
            surplus = surplus - more
    return np.array(counts)


def scatter_about(stream_key, shape, scale, reach, split=(), kind=jnp.bfloat16):
    values = jax.random.normal(stream_key, shape, jnp.float32) * scale
    if len(split) > 0:
        values = steps_of(stream_key, shape, split, -0.22, 0.18) * values
    return jnp.clip(values, min=-reach, max=reach).astype(kind)


def setup_inputs(seed: int = 0) -> dict:
    key_list = jax.random.split(jax.random.key(seed), 7)
    tokens = scatter_about(key_list[0], (STEPS, TOKENS, D), 1.0, 6.0, ((1, 256),))
    expert_ids_keys = jax.random.split(jax.random.fold_in(key_list[1], 1), STEPS * TOKENS // ROWS_DEV)
    expert_ids_turns = jax.random.permutation(jax.random.fold_in(key_list[1], 3), STEPS * TOKENS // ROWS_DEV)
    expert_ids = jax.vmap(lambda own, number: routed_block(jax.random.fold_in(key_list[1], 2), own, number, ROWS_DEV, EXPERTS, TOP, CAP, 2))(expert_ids_keys, expert_ids_turns).reshape((STEPS, TOKENS, TOP))
    gate_probs = jnp.clip(0.1 + 0.9 * jax.random.uniform(key_list[2], (STEPS, TOKENS, TOP), jnp.float32) ** steps_of(key_list[2], (STEPS, TOKENS, TOP), ((1, 256),), -0.2, 0.2), 0.1, 1.0)
    gate_up = scatter_about(key_list[3], (EXPERTS, 2, FF, D), D ** -0.5, 0.09375, ((0, 64), (2, 4)))
    down_proj = scatter_about(key_list[4], (EXPERTS, FF, D), FF ** -0.5, 0.21875, ((0, 64), (1, 4)))
    pairs = draw_pairs(jax.random.fold_in(key_list[6], 71), 0)
    return {"tokens": tokens, "expert_ids": expert_ids, "gate_probs": gate_probs, "gate_up": gate_up, "down_proj": down_proj, "pairs": pairs}


def expert_rows(row_block, expert_gu, expert_down):
    dims = (((1,), (1,)), ((), ()))
    gate = lax.dot_general(row_block, expert_gu[0], dims, preferred_element_type=jnp.float32)
    upper = lax.dot_general(row_block, expert_gu[1], dims, preferred_element_type=jnp.float32)
    hidden = (jax.nn.silu(gate) * upper).astype(jnp.bfloat16)
    quarter = FF // N_DP
    total = jnp.zeros((row_block.shape[0], D), jnp.float32)
    for q_index in range(N_DP):
        piece = jnp.dot(hidden[:, q_index * quarter:(q_index + 1) * quarter],
                        expert_down[q_index * quarter:(q_index + 1) * quarter],
                        preferred_element_type=jnp.float32).astype(jnp.bfloat16)
        total = total + piece.astype(jnp.float32)
    return total.astype(jnp.bfloat16)


def one_step(step_tokens, step_ids, step_gates, gate_up, down_proj):
    flat_ids = step_ids.reshape(-1)
    flat_gates = step_gates.reshape(-1)
    slot_total = (TOKENS // ROWS_DEV) * CAP

    def per_expert(accum, expert_index):
        hit_mask = flat_ids == expert_index
        entry_idx = jnp.nonzero(hit_mask, size=slot_total, fill_value=0)[0].astype(jnp.int32)
        hit_count = jnp.sum(hit_mask.astype(jnp.int32))
        valid = jnp.arange(slot_total, dtype=jnp.int32) < hit_count
        token_idx = entry_idx // TOP
        row_block = jnp.take(step_tokens, token_idx, axis=0)
        expert_out = expert_rows(row_block, gate_up[expert_index], down_proj[expert_index])
        weights = jnp.where(valid, jnp.take(flat_gates, entry_idx), jnp.zeros((), flat_gates.dtype))
        accum = accum.at[token_idx].add(weights[:, None] * expert_out.astype(jnp.float32))
        return accum, None

    accum, _ = lax.scan(per_expert, jnp.zeros((TOKENS, D), jnp.float32), jnp.arange(EXPERTS, dtype=jnp.int32))
    return accum.astype(jnp.bfloat16)


def reference(tokens, expert_ids, gate_probs, gate_up, down_proj, pairs):
    results = jnp.stack([one_step(tokens[step_idx], expert_ids[step_idx], gate_probs[step_idx], gate_up, down_proj)
                         for step_idx in range(STEPS)])
    positions = jnp.arange(EXPERTS, dtype=jnp.int32)
    lower_dev = pairs[:, 0].astype(jnp.int32)
    upper_dev = pairs[:, 1].astype(jnp.int32)
    sigma = positions + jnp.sum(jnp.where(positions[:, None] == lower_dev[None, :], (upper_dev - lower_dev)[None, :], 0), axis=1)
    sigma = sigma + jnp.sum(jnp.where(positions[:, None] == upper_dev[None, :], (lower_dev - upper_dev)[None, :], 0), axis=1)
    sigma = sigma.astype(jnp.int32)
    return results, jnp.take(gate_up, sigma, axis=0), jnp.take(down_proj, sigma, axis=0)
```

```python
import jax
import jax.numpy as jnp
from jax import lax
from jax.experimental import pallas as pl
from jax.experimental.pallas import tpu as pltpu
from jax.sharding import Mesh, PartitionSpec as P


F32 = jnp.float32
BF16 = jnp.bfloat16
CAP = 3
CHUNK = 1024
META = 128


def ffn_kernel(n_in, x_ref, gu_a, gu_b, dn_a, dn_b, out_ref, acc, hid):
    step = pl.program_id(0)
    rows = x_ref.shape[0]
    units = hid.shape[1]
    tile = 256

    @pl.when(step < n_in)
    def _():
        weights = jnp.concatenate([gu_a[0, 0], gu_b[0, 0], gu_a[0, 1], gu_b[0, 1]], axis=0)

        def body(m, carry):
            at = pl.ds(pl.multiple_of(m * tile, tile), tile)
            part = lax.dot_general(
                x_ref[at, :], weights, (((1,), (1,)), ((), ())), preferred_element_type=F32
            )

            @pl.when(step == 0)
            def _():
                acc[at, :] = part

            @pl.when(step > 0)
            def _():
                acc[at, :] += part

            return carry

        lax.fori_loop(0, rows // tile, body, 0)

    @pl.when(step == n_in - 1)
    def _():
        def body(m, carry):
            at = pl.ds(pl.multiple_of(m * tile, tile), tile)
            gate = acc[at, :units]
            hid[at, :] = (gate / (1.0 + jnp.exp(-gate)) * acc[at, units:]).astype(BF16)
            return carry

        lax.fori_loop(0, rows // tile, body, 0)

    @pl.when(step >= n_in)
    def _():
        weights = jnp.concatenate([dn_a[0], dn_b[0]], axis=0)

        def body(m, carry):
            at = pl.ds(pl.multiple_of(m * tile, tile), tile)
            out_ref[at, :] = jnp.dot(hid[at, :], weights, preferred_element_type=F32).astype(BF16)
            return carry

        lax.fori_loop(0, rows // tile, body, 0)


def ffn(x, gu_a, gu_b, dn_a, dn_b):
    rows, depth = x.shape
    units = gu_a.shape[2]
    n_in = depth // CHUNK

    def first(i):
        return jnp.minimum(i, n_in - 1)

    def second(i):
        return jnp.maximum(i - n_in, 0)

    gu_spec = pl.BlockSpec((1, 2, units, CHUNK), lambda i: (0, 0, 0, first(i)))
    dn_spec = pl.BlockSpec((1, units, CHUNK), lambda i: (0, 0, second(i)))
    flops = 2 * rows * depth * units * 2 * 3
    traffic = 2 * (2 * rows * depth + 6 * units * depth)
    return pl.pallas_call(
        lambda *refs: ffn_kernel(n_in, *refs),
        grid=(2 * n_in,),
        in_specs=[
            pl.BlockSpec((rows, CHUNK), lambda i: (0, first(i))),
            gu_spec,
            gu_spec,
            dn_spec,
            dn_spec,
        ],
        out_specs=pl.BlockSpec((rows, CHUNK), lambda i: (0, second(i))),
        out_shape=jax.ShapeDtypeStruct((rows, depth), BF16),
        scratch_shapes=[
            pltpu.VMEM((rows, 4 * units), F32),
            pltpu.VMEM((rows, 2 * units), BF16),
        ],
        cost_estimate=pl.CostEstimate(
            flops=flops, bytes_accessed=traffic, transcendentals=rows * units * 2
        ),
        name="ffn",
    )(x, gu_a, gu_b, dn_a, dn_b)


def swap(value, axes):
    count = 2 ** len(axes)
    return lax.ppermute(value, axes, [(i, i ^ (count - 1)) for i in range(count)])


def local(tokens, expert_ids, gate_probs, gate_up, down_proj, pairs):
    steps, rows, depth = tokens.shape
    tops = expert_ids.shape[2]
    plane = lax.axis_index("h")
    slot = (
        (lax.axis_index("x") * 4 + lax.axis_index("y")) * 2 + plane
    ) * 2 + lax.axis_index("c")
    own = steps * rows
    total = 4 * own
    experts = 32
    per = 4 * steps * CAP
    slots = experts * per

    gates = gate_probs.reshape(own, tops)
    high = lax.reduce_precision(gates, 8, 7)
    low = gates - high
    ext = jnp.concatenate(
        [
            tokens.reshape(own, depth),
            expert_ids.reshape(own, tops).astype(BF16),
            high.astype(BF16),
            low.astype(BF16),
            jnp.zeros((own, META - 3 * tops), BF16),
        ],
        axis=1,
    )
    column = [ext, swap(ext, ("h",)), swap(ext, ("qh",)), swap(ext, ("qh", "h"))]
    gu_b, dn_b = swap((gate_up, down_proj), ("ql",))
    got_gu, got_dn = lax.ppermute(
        (gate_up, down_proj), ("x",), [(i, i ^ 2) for i in range(4)]
    )

    held = jnp.concatenate(column, axis=0)
    meta = held[:, depth:].astype(F32)
    ids = meta[:, :tops]
    e_pos = lax.iota(jnp.int32, experts)
    e_num = (((e_pos >> 1) * 2 + plane) * 2 + (e_pos & 1)).astype(F32)
    hit = ids[:, :, None] == e_num
    named = jnp.any(hit, axis=1)
    g_high = jnp.sum(jnp.where(hit, meta[:, tops : 2 * tops, None], 0.0), axis=1).astype(BF16)
    g_low = jnp.sum(jnp.where(hit, meta[:, 2 * tops : 3 * tops, None], 0.0), axis=1).astype(BF16)
    t_row = lax.broadcasted_iota(jnp.int32, (total, total), 0)
    t_col = lax.broadcasted_iota(jnp.int32, (total, total), 1)
    earlier = ((t_row // rows == t_col // rows) & (t_col < t_row)).astype(BF16)
    rank = jnp.dot(earlier, named.astype(BF16), preferred_element_type=F32)
    place = jnp.where(named, rank, -1.0).astype(BF16)
    spread = (
        lax.broadcasted_iota(jnp.int32, (experts, slots), 0)
        == lax.broadcasted_iota(jnp.int32, (experts, slots), 1) // per
    ).astype(BF16)
    wide = jnp.dot(
        jnp.concatenate([place, g_high, g_low], axis=0), spread, preferred_element_type=F32
    )
    n_col = lax.broadcasted_iota(jnp.int32, (total, slots), 1) % per
    t_blk = lax.broadcasted_iota(jnp.int32, (total, slots), 0) // rows
    chosen = (n_col // CAP == t_blk) & (wide[:total] == (n_col % CAP).astype(F32))
    pick = chosen.astype(BF16)
    mix_high = jnp.where(chosen, wide[total : 2 * total], 0.0).astype(BF16)
    mix_low = jnp.where(chosen, wide[2 * total :], 0.0).astype(BF16)

    packed = lax.dot_general(
        pick, held[:, :depth], (((0,), (0,)), ((), ())), preferred_element_type=F32
    ).astype(BF16)
    arrived = lax.all_to_all(
        packed.reshape(experts, per, depth), ("x", "y", "c"), 0, 0, tiled=True
    ).reshape(slots, depth)
    made = ffn(arrived, gate_up, gu_b, down_proj, dn_b)
    back = lax.all_to_all(
        made.reshape(experts, per, depth), ("x", "y", "c"), 0, 0, tiled=True
    ).reshape(slots, depth)
    mixed = jnp.dot(mix_high, back, preferred_element_type=F32) + jnp.dot(
        mix_low, back, preferred_element_type=F32
    )
    parts = mixed.reshape(4, own, depth)
    others = parts[1:].astype(BF16)
    total_out = (
        parts[0]
        + swap(others[0], ("h",)).astype(F32)
        + swap(others[1], ("qh",)).astype(F32)
        + swap(others[2], ("qh", "h")).astype(F32)
    )
    moving = jnp.any(pairs == slot)
    return (
        total_out.astype(BF16).reshape(steps, rows, depth),
        jnp.where(moving, got_gu, gate_up),
        jnp.where(moving, got_dn, down_proj),
    )


def solution(mesh):
    fine = Mesh(mesh.devices.reshape(2, 2, 4, 4, 2, 2), ("qh", "ql", "x", "y", "h", "c"))
    dp = ("qh", "ql")
    ex = ("x", "y", "h", "c")
    return jax.shard_map(
        local,
        mesh=fine,
        in_specs=(
            P(None, dp + ex, None),
            P(None, dp + ex, None),
            P(None, dp + ex, None),
            P(ex, None, dp, None),
            P(ex, dp, None),
            P(),
        ),
        out_specs=(
            P(None, dp + ex, None),
            P(ex, None, dp, None),
            P(ex, dp, None),
        ),
        check_vma=False,
    )
```

```python
import jax
import jax.numpy as jnp
from jax import lax
from jax.experimental import pallas as pl
from jax.experimental.pallas import tpu as pltpu
from jax.sharding import Mesh, PartitionSpec as P


F32 = jnp.float32
BF16 = jnp.bfloat16
CAP = 3
CHUNK = 1024
META = 128
TILE = 256
PLANE = ("x", "y", "c")


def over_tiles(rows, body):
    def wrapped(m, carry):
        body(pl.ds(pl.multiple_of(m * TILE, TILE), TILE))
        return carry

    lax.fori_loop(0, rows // TILE, wrapped, 0)


def up_first_kernel(x_ref, gu_a, gu_b, acc):
    step = pl.program_id(0)
    weights = jnp.concatenate([gu_a[0, 0], gu_b[0, 0], gu_a[0, 1], gu_b[0, 1]], axis=0)

    def body(at):
        part = lax.dot_general(
            x_ref[at, :], weights, (((1,), (1,)), ((), ())), preferred_element_type=F32
        )

        @pl.when(step == 0)
        def _():
            acc[at, :] = part

        @pl.when(step > 0)
        def _():
            acc[at, :] += part

    over_tiles(x_ref.shape[0], body)


def up_last_kernel(n_in, x_ref, gu_a, gu_b, start, hid, acc):
    step = pl.program_id(0)
    units = hid.shape[1]
    weights = jnp.concatenate([gu_a[0, 0], gu_b[0, 0], gu_a[0, 1], gu_b[0, 1]], axis=0)

    def body(at):
        part = lax.dot_general(
            x_ref[at, :], weights, (((1,), (1,)), ((), ())), preferred_element_type=F32
        )

        @pl.when(step == 0)
        def _():
            acc[at, :] = start[at, :] + part

        @pl.when(step > 0)
        def _():
            acc[at, :] += part

        @pl.when(step == n_in - 1)
        def _():
            gate = acc[at, :units]
            hid[at, :] = (gate / (1.0 + jnp.exp(-gate)) * acc[at, units:]).astype(BF16)

    over_tiles(x_ref.shape[0], body)


def up(x, gu_a, gu_b, at_col, start=None):
    rows, depth = x.shape
    units = gu_a.shape[2]
    n_in = depth // CHUNK
    base = at_col // CHUNK
    gu_spec = pl.BlockSpec((1, 2, units, CHUNK), lambda i: (0, 0, 0, base + i))
    specs = [pl.BlockSpec((rows, CHUNK), lambda i: (0, i)), gu_spec, gu_spec]
    cost = pl.CostEstimate(
        flops=2 * rows * depth * units * 4,
        bytes_accessed=2 * rows * depth + 8 * units * depth + 16 * rows * units,
        transcendentals=0,
    )
    wide = pl.BlockSpec((rows, 4 * units), lambda i: (0, 0))
    if start is None:
        return pl.pallas_call(
            up_first_kernel,
            grid=(n_in,),
            in_specs=specs,
            out_specs=wide,
            out_shape=jax.ShapeDtypeStruct((rows, 4 * units), F32),
            cost_estimate=cost,
            name="up_first",
        )(x, gu_a, gu_b)
    return pl.pallas_call(
        lambda *refs: up_last_kernel(n_in, *refs),
        grid=(n_in,),
        in_specs=specs + [wide],
        out_specs=pl.BlockSpec((rows, 2 * units), lambda i: (0, 0)),
        out_shape=jax.ShapeDtypeStruct((rows, 2 * units), BF16),
        scratch_shapes=[pltpu.VMEM((rows, 4 * units), F32)],
        cost_estimate=cost,
        name="up_last",
    )(x, gu_a, gu_b, start)


def down_kernel(hid_a, hid_b, w0, w1, w2, w3, out_ref):
    weights = jnp.concatenate([w0[...], w1[...], w2[...], w3[...]], axis=0)

    def body(at):
        hidden = jnp.concatenate([hid_a[at, :], hid_b[at, :]], axis=1)
        out_ref[at, :] = jnp.dot(hidden, weights, preferred_element_type=F32).astype(BF16)

    over_tiles(hid_a.shape[0], body)


def down(hid_a, hid_b, pieces):
    rows, units = hid_a.shape
    shard, depth = pieces[0].shape
    hid_spec = pl.BlockSpec((rows, units), lambda i: (0, 0))
    w_spec = pl.BlockSpec((shard, CHUNK), lambda i: (0, i))
    return pl.pallas_call(
        down_kernel,
        grid=(depth // CHUNK,),
        in_specs=[hid_spec, hid_spec] + [w_spec] * 4,
        out_specs=pl.BlockSpec((rows, CHUNK), lambda i: (0, i)),
        out_shape=jax.ShapeDtypeStruct((rows, depth), BF16),
        cost_estimate=pl.CostEstimate(
            flops=2 * rows * depth * units * 2,
            bytes_accessed=2 * rows * depth + 8 * shard * depth + 4 * rows * units,
            transcendentals=0,
        ),
        name="down",
    )(hid_a, hid_b, *pieces)


def swap(value, axes):
    count = 2 ** len(axes)
    return lax.ppermute(value, axes, [(i, i ^ (count - 1)) for i in range(count)])


def column(own):
    return jnp.concatenate(
        [own, swap(own, ("h",)), swap(own, ("qh",)), swap(own, ("qh", "h"))], axis=0
    )


def tables(meta, rows, tops, plane, q_high, experts, slots):
    total = meta.shape[0]
    per = slots // experts
    ids = meta[:, :tops]
    e_pos = lax.iota(jnp.int32, experts)
    e_num = (((e_pos >> 1) * 2 + plane) * 2 + (e_pos & 1)).astype(F32)
    hit = ids[:, :, None] == e_num
    named = jnp.any(hit, axis=1)
    g_high = jnp.sum(jnp.where(hit, meta[:, tops : 2 * tops, None], 0.0), axis=1).astype(BF16)
    g_low = jnp.sum(jnp.where(hit, meta[:, 2 * tops : 3 * tops, None], 0.0), axis=1).astype(BF16)
    t_row = lax.broadcasted_iota(jnp.int32, (total, total), 0)
    t_col = lax.broadcasted_iota(jnp.int32, (total, total), 1)
    earlier = ((t_row // rows == t_col // rows) & (t_col < t_row)).astype(BF16)
    rank = jnp.dot(earlier, named.astype(BF16), preferred_element_type=F32)
    place = jnp.where(named, rank, -1.0).astype(BF16)
    spread = (
        lax.broadcasted_iota(jnp.int32, (experts, slots), 0)
        == lax.broadcasted_iota(jnp.int32, (experts, slots), 1) // per
    ).astype(BF16)
    wide = jnp.dot(
        jnp.concatenate([place, g_high, g_low], axis=0), spread, preferred_element_type=F32
    )
    n_col = lax.broadcasted_iota(jnp.int32, (total, slots), 1) % per
    t_blk = lax.broadcasted_iota(jnp.int32, (total, slots), 0) // rows
    t_blk = t_blk ^ (q_high * (total // rows // 2))
    chosen = (n_col // CAP == t_blk) & (wide[:total] == (n_col % CAP).astype(F32))
    mix = jnp.concatenate(
        [
            jnp.where(chosen, wide[total : 2 * total], 0.0),
            jnp.where(chosen, wide[2 * total :], 0.0),
        ],
        axis=0,
    )
    return chosen.astype(BF16), mix.astype(BF16)


def pack(pick, held):
    return lax.dot_general(
        pick, held, (((0,), (0,)), ((), ())), preferred_element_type=F32
    ).astype(BF16)


def across(value, experts):
    slots, depth = value.shape
    return lax.all_to_all(
        value.reshape(experts, slots // experts, depth), PLANE, 0, 0, tiled=True
    ).reshape(slots, depth)


def local(tokens, expert_ids, gate_probs, gate_up, down_proj, pairs):
    steps, rows, depth = tokens.shape
    tops = expert_ids.shape[2]
    half = depth // 2
    plane = lax.axis_index("h")
    q_high = lax.axis_index("qh")
    slot = (
        (lax.axis_index("x") * 4 + lax.axis_index("y")) * 2 + plane
    ) * 2 + lax.axis_index("c")
    own = steps * rows
    experts = 32
    slots = experts * 4 * steps * CAP

    flat = tokens.reshape(own, depth)
    gates = gate_probs.reshape(own, tops)
    high = lax.reduce_precision(gates, 8, 7)
    low = gates - high
    first = jnp.concatenate(
        [
            flat[:, :half],
            expert_ids.reshape(own, tops).astype(BF16),
            high.astype(BF16),
            low.astype(BF16),
            jnp.zeros((own, META - 3 * tops), BF16),
        ],
        axis=1,
    )
    across_x = [(i, i ^ 2) for i in range(4)]
    got_dn = lax.ppermute(down_proj, ("x",), across_x)
    held0 = column(first)
    held1 = column(flat[:, half:])
    gu_b = swap(gate_up, ("ql",))
    mine = lax.dynamic_slice_in_dim(down_proj[0], q_high * half, half, axis=1)
    theirs = lax.dynamic_slice_in_dim(down_proj[0], (1 - q_high) * half, half, axis=1)
    pieces = [
        mine,
        swap(mine, ("ql",)),
        swap(theirs, ("qh",)),
        swap(theirs, ("qh", "ql")),
    ]

    pick, mix = tables(
        held0[:, half:].astype(F32), rows, tops, plane, q_high, experts, slots
    )
    packed0 = pack(pick, held0[:, :half])
    x0 = across(packed0, experts)
    packed1 = pack(pick, held1)
    x1 = across(packed1, experts)
    start = up(x0, gate_up, gu_b, 0)
    hidden = up(x1, gate_up, gu_b, half, start)
    hidden_b = swap(hidden, ("qh",))
    got_gu = lax.ppermute(gate_up, ("x",), across_x)
    made = down(hidden, hidden_b, pieces)
    back = across(made, experts)
    both = jnp.dot(mix, back, preferred_element_type=F32)
    mixed = both[: 4 * own] + both[4 * own :]
    parts = mixed.reshape(4, own, half)
    sent = parts[1:].astype(BF16)
    near = parts[0] + swap(sent[0], ("h",)).astype(F32)
    far = swap(sent[1], ("qh",)).astype(F32) + swap(sent[2], ("qh", "h")).astype(F32)
    low_half = q_high == 0
    out = jnp.concatenate(
        [jnp.where(low_half, near, far), jnp.where(low_half, far, near)], axis=1
    )
    moving = jnp.any(pairs == slot)
    return (
        out.astype(BF16).reshape(steps, rows, depth),
        jnp.where(moving, got_gu, gate_up),
        jnp.where(moving, got_dn, down_proj),
    )


def solution(mesh):
    fine = Mesh(mesh.devices.reshape(2, 2, 4, 4, 2, 2), ("qh", "ql", "x", "y", "h", "c"))
    dp = ("qh", "ql")
    ex = ("x", "y", "h", "c")
    return jax.shard_map(
        local,
        mesh=fine,
        in_specs=(
            P(None, dp + ex, None),
            P(None, dp + ex, None),
            P(None, dp + ex, None),
            P(ex, None, dp, None),
            P(ex, dp, None),
            P(),
        ),
        out_specs=(
            P(None, dp + ex, None),
            P(ex, None, dp, None),
            P(ex, dp, None),
        ),
        check_vma=False,
    )
```

```python
import jax
import jax.numpy as jnp
from jax import lax
from jax.experimental import pallas as pl
from jax.experimental.pallas import tpu as pltpu
from jax.sharding import Mesh, PartitionSpec as P


F32 = jnp.float32
BF16 = jnp.bfloat16
CAP = 3
CHUNK = 1024
META = 128
TILE = 256
PLANE = ("x", "y", "c")


def over_tiles(rows, body):
    def wrapped(m, carry):
        body(pl.ds(pl.multiple_of(m * TILE, TILE), TILE))
        return carry

    lax.fori_loop(0, rows // TILE, wrapped, 0)


def up_first_kernel(x_ref, gu_a, gu_b, acc):
    step = pl.program_id(0)
    weights = jnp.concatenate([gu_a[0, 0], gu_b[0, 0], gu_a[0, 1], gu_b[0, 1]], axis=0)

    def body(at):
        part = lax.dot_general(
            x_ref[at, :], weights, (((1,), (1,)), ((), ())), preferred_element_type=F32
        )

        @pl.when(step == 0)
        def _():
            acc[at, :] = part

        @pl.when(step > 0)
        def _():
            acc[at, :] += part

    over_tiles(x_ref.shape[0], body)


def up_last_kernel(n_in, x_ref, gu_a, gu_b, start, hid, acc):
    step = pl.program_id(0)
    units = hid.shape[1]
    weights = jnp.concatenate([gu_a[0, 0], gu_b[0, 0], gu_a[0, 1], gu_b[0, 1]], axis=0)

    def body(at):
        part = lax.dot_general(
            x_ref[at, :], weights, (((1,), (1,)), ((), ())), preferred_element_type=F32
        )

        @pl.when(step == 0)
        def _():
            acc[at, :] = start[at, :] + part

        @pl.when(step > 0)
        def _():
            acc[at, :] += part

        @pl.when(step == n_in - 1)
        def _():
            gate = acc[at, :units]
            hid[at, :] = (gate / (1.0 + jnp.exp(-gate)) * acc[at, units:]).astype(BF16)

    over_tiles(x_ref.shape[0], body)


def up(x, gu_a, gu_b, at_col, start=None):
    rows, depth = x.shape
    units = gu_a.shape[2]
    n_in = depth // CHUNK
    base = at_col // CHUNK
    gu_spec = pl.BlockSpec((1, 2, units, CHUNK), lambda i: (0, 0, 0, base + i))
    specs = [pl.BlockSpec((rows, CHUNK), lambda i: (0, i)), gu_spec, gu_spec]
    cost = pl.CostEstimate(
        flops=2 * rows * depth * units * 4,
        bytes_accessed=2 * rows * depth + 8 * units * depth + 16 * rows * units,
        transcendentals=0,
    )
    wide = pl.BlockSpec((rows, 4 * units), lambda i: (0, 0))
    if start is None:
        return pl.pallas_call(
            up_first_kernel,
            grid=(n_in,),
            in_specs=specs,
            out_specs=wide,
            out_shape=jax.ShapeDtypeStruct((rows, 4 * units), F32),
            cost_estimate=cost,
            name="up_first",
        )(x, gu_a, gu_b)
    return pl.pallas_call(
        lambda *refs: up_last_kernel(n_in, *refs),
        grid=(n_in,),
        in_specs=specs + [wide],
        out_specs=pl.BlockSpec((rows, 2 * units), lambda i: (0, 0)),
        out_shape=jax.ShapeDtypeStruct((rows, 2 * units), BF16),
        scratch_shapes=[pltpu.VMEM((rows, 4 * units), F32)],
        cost_estimate=cost,
        name="up_last",
    )(x, gu_a, gu_b, start)


def down_kernel(hid_a, hid_b, w0, w1, w2, w3, out_ref):
    weights = jnp.concatenate([w0[...], w1[...], w2[...], w3[...]], axis=0)

    def body(at):
        hidden = jnp.concatenate([hid_a[at, :], hid_b[at, :]], axis=1)
        out_ref[at, :] = jnp.dot(hidden, weights, preferred_element_type=F32).astype(BF16)

    over_tiles(hid_a.shape[0], body)


def down(hid_a, hid_b, pieces):
    rows, units = hid_a.shape
    shard, depth = pieces[0].shape
    hid_spec = pl.BlockSpec((rows, units), lambda i: (0, 0))
    w_spec = pl.BlockSpec((shard, CHUNK), lambda i: (0, i))
    return pl.pallas_call(
        down_kernel,
        grid=(depth // CHUNK,),
        in_specs=[hid_spec, hid_spec] + [w_spec] * 4,
        out_specs=pl.BlockSpec((rows, CHUNK), lambda i: (0, i)),
        out_shape=jax.ShapeDtypeStruct((rows, depth), BF16),
        cost_estimate=pl.CostEstimate(
            flops=2 * rows * depth * units * 2,
            bytes_accessed=2 * rows * depth + 8 * shard * depth + 4 * rows * units,
            transcendentals=0,
        ),
        name="down",
    )(hid_a, hid_b, *pieces)


def swap(value, axes):
    count = 2 ** len(axes)
    return lax.ppermute(value, axes, [(i, i ^ (count - 1)) for i in range(count)])


def column(own):
    return jnp.concatenate(
        [own, swap(own, ("h",)), swap(own, ("qh",)), swap(own, ("qh", "h"))], axis=0
    )


def tables(meta, rows, tops, plane, q_high, experts, slots):
    total = meta.shape[0]
    per = slots // experts
    ids = meta[:, :tops]
    e_pos = lax.iota(jnp.int32, experts)
    e_num = (((e_pos >> 1) * 2 + plane) * 2 + (e_pos & 1)).astype(F32)
    hit = ids[:, :, None] == e_num
    named = jnp.any(hit, axis=1)
    g_high = jnp.sum(jnp.where(hit, meta[:, tops : 2 * tops, None], 0.0), axis=1).astype(BF16)
    g_low = jnp.sum(jnp.where(hit, meta[:, 2 * tops : 3 * tops, None], 0.0), axis=1).astype(BF16)
    t_row = lax.broadcasted_iota(jnp.int32, (total, total), 0)
    t_col = lax.broadcasted_iota(jnp.int32, (total, total), 1)
    earlier = ((t_row // rows == t_col // rows) & (t_col < t_row)).astype(BF16)
    rank = jnp.dot(earlier, named.astype(BF16), preferred_element_type=F32)
    place = jnp.where(named, rank, -1.0).astype(BF16)
    spread = (
        lax.broadcasted_iota(jnp.int32, (experts, slots), 0)
        == lax.broadcasted_iota(jnp.int32, (experts, slots), 1) // per
    ).astype(BF16)
    wide = jnp.dot(
        jnp.concatenate([place, g_high, g_low], axis=0), spread, preferred_element_type=F32
    )
    n_col = lax.broadcasted_iota(jnp.int32, (total, slots), 1) % per
    t_blk = lax.broadcasted_iota(jnp.int32, (total, slots), 0) // rows
    t_blk = t_blk ^ (q_high * (total // rows // 2))
    chosen = (n_col // CAP == t_blk) & (wide[:total] == (n_col % CAP).astype(F32))
    mix = jnp.concatenate(
        [
            jnp.where(chosen, wide[total : 2 * total], 0.0),
            jnp.where(chosen, wide[2 * total :], 0.0),
        ],
        axis=0,
    )
    return chosen.astype(BF16), mix.astype(BF16)


def pack(pick, held):
    return lax.dot_general(
        pick, held, (((0,), (0,)), ((), ())), preferred_element_type=F32
    ).astype(BF16)


def across(value, experts):
    slots, depth = value.shape
    return lax.all_to_all(
        value.reshape(experts, slots // experts, depth), PLANE, 0, 0, tiled=True
    ).reshape(slots, depth)


def local(tokens, expert_ids, gate_probs, gate_up, down_proj, pairs):
    steps, rows, depth = tokens.shape
    tops = expert_ids.shape[2]
    half = depth // 2
    plane = lax.axis_index("h")
    q_high = lax.axis_index("qh")
    slot = (
        (lax.axis_index("x") * 4 + lax.axis_index("y")) * 2 + plane
    ) * 2 + lax.axis_index("c")
    own = steps * rows
    experts = 32
    slots = experts * 4 * steps * CAP

    flat = tokens.reshape(own, depth)
    gates = gate_probs.reshape(own, tops)
    high = lax.reduce_precision(gates, 8, 7)
    low = gates - high
    first = jnp.concatenate(
        [
            flat[:, :half],
            expert_ids.reshape(own, tops).astype(BF16),
            high.astype(BF16),
            low.astype(BF16),
            jnp.zeros((own, META - 3 * tops), BF16),
        ],
        axis=1,
    )
    across_x = [(i, i ^ 2) for i in range(4)]
    got_dn = lax.ppermute(down_proj, ("x",), across_x)
    held0 = column(first)
    later, _ = lax.optimization_barrier((flat, held0[:8, :META]))
    held1 = column(later[:, half:])
    gu_b = swap(gate_up, ("ql",))
    mine = lax.dynamic_slice_in_dim(down_proj[0], q_high * half, half, axis=1)
    theirs = lax.dynamic_slice_in_dim(down_proj[0], (1 - q_high) * half, half, axis=1)
    near_piece = swap(mine, ("ql",))
    pieces = [mine, near_piece, swap(theirs, ("qh",)), swap(theirs, ("qh", "ql"))]

    pick, mix = tables(
        held0[:, half:].astype(F32), rows, tops, plane, q_high, experts, slots
    )
    packed0 = pack(pick, held0[:, :half])
    x0 = across(packed0, experts)
    packed1 = pack(pick, held1)
    x1 = across(packed1, experts)
    start = up(x0, gate_up, gu_b, 0)
    hidden = up(x1, gate_up, gu_b, half, start)
    hidden_b = swap(hidden, ("qh",))
    got_gu = lax.ppermute(gate_up, ("x",), across_x)
    made = down(hidden, hidden_b, pieces)
    back = across(made, experts)
    both = jnp.dot(mix, back, preferred_element_type=F32)
    mixed = both[: 4 * own] + both[4 * own :]
    parts = mixed.reshape(4, own, half)
    sent = parts[1:].astype(BF16)
    near = parts[0] + swap(sent[0], ("h",)).astype(F32)
    far = swap(sent[1], ("qh",)).astype(F32) + swap(sent[2], ("qh", "h")).astype(F32)
    low_half = q_high == 0
    out = jnp.concatenate(
        [jnp.where(low_half, near, far), jnp.where(low_half, far, near)], axis=1
    )
    moving = jnp.any(pairs == slot)
    return (
        out.astype(BF16).reshape(steps, rows, depth),
        jnp.where(moving, got_gu, gate_up),
        jnp.where(moving, got_dn, down_proj),
    )


def solution(mesh):
    fine = Mesh(mesh.devices.reshape(2, 2, 4, 4, 2, 2), ("qh", "ql", "x", "y", "h", "c"))
    dp = ("qh", "ql")
    ex = ("x", "y", "h", "c")
    return jax.shard_map(
        local,
        mesh=fine,
        in_specs=(
            P(None, dp + ex, None),
            P(None, dp + ex, None),
            P(None, dp + ex, None),
            P(ex, None, dp, None),
            P(ex, dp, None),
            P(),
        ),
        out_specs=(
            P(None, dp + ex, None),
            P(ex, None, dp, None),
            P(ex, dp, None),
        ),
        check_vma=False,
    )
```

```python
import jax
import jax.numpy as jnp
from jax import lax
from jax.experimental import pallas as pl
from jax.experimental.pallas import tpu as pltpu
from jax.sharding import Mesh, PartitionSpec as P


F32 = jnp.float32
BF16 = jnp.bfloat16
CAP = 3
CHUNK = 1024
META = 128
HEAD = 256
TILE = 256
PLANE = ("x", "y", "c")


def over_tiles(rows, body):
    def wrapped(m, carry):
        body(pl.ds(pl.multiple_of(m * TILE, TILE), TILE))
        return carry

    lax.fori_loop(0, rows // TILE, wrapped, 0)


def up_first_kernel(x_ref, gu_a, gu_b, acc):
    step = pl.program_id(0)
    weights = jnp.concatenate([gu_a[0, 0], gu_b[0, 0], gu_a[0, 1], gu_b[0, 1]], axis=0)

    def body(at):
        part = lax.dot_general(
            x_ref[at, :], weights, (((1,), (1,)), ((), ())), preferred_element_type=F32
        )

        @pl.when(step == 0)
        def _():
            acc[at, :] = part

        @pl.when(step > 0)
        def _():
            acc[at, :] += part

    over_tiles(x_ref.shape[0], body)


def up_last_kernel(n_in, x_ref, gu_a, gu_b, start, hid, acc):
    step = pl.program_id(0)
    units = hid.shape[1]
    weights = jnp.concatenate([gu_a[0, 0], gu_b[0, 0], gu_a[0, 1], gu_b[0, 1]], axis=0)

    def body(at):
        part = lax.dot_general(
            x_ref[at, :], weights, (((1,), (1,)), ((), ())), preferred_element_type=F32
        )

        @pl.when(step == 0)
        def _():
            acc[at, :] = start[at, :] + part

        @pl.when(step > 0)
        def _():
            acc[at, :] += part

        @pl.when(step == n_in - 1)
        def _():
            gate = acc[at, :units]
            hid[at, :] = (gate / (1.0 + jnp.exp(-gate)) * acc[at, units:]).astype(BF16)

    over_tiles(x_ref.shape[0], body)


def up(x, gu_a, gu_b, at_col, start=None):
    rows, depth = x.shape
    units = gu_a.shape[2]
    n_in = depth // CHUNK
    base = at_col // CHUNK
    gu_spec = pl.BlockSpec((1, 2, units, CHUNK), lambda i: (0, 0, 0, base + i))
    specs = [pl.BlockSpec((rows, CHUNK), lambda i: (0, i)), gu_spec, gu_spec]
    cost = pl.CostEstimate(
        flops=2 * rows * depth * units * 4,
        bytes_accessed=2 * rows * depth + 8 * units * depth + 16 * rows * units,
        transcendentals=0,
    )
    wide = pl.BlockSpec((rows, 4 * units), lambda i: (0, 0))
    if start is None:
        return pl.pallas_call(
            up_first_kernel,
            grid=(n_in,),
            in_specs=specs,
            out_specs=wide,
            out_shape=jax.ShapeDtypeStruct((rows, 4 * units), F32),
            cost_estimate=cost,
            name="up_first",
        )(x, gu_a, gu_b)
    return pl.pallas_call(
        lambda *refs: up_last_kernel(n_in, *refs),
        grid=(n_in,),
        in_specs=specs + [wide],
        out_specs=pl.BlockSpec((rows, 2 * units), lambda i: (0, 0)),
        out_shape=jax.ShapeDtypeStruct((rows, 2 * units), BF16),
        scratch_shapes=[pltpu.VMEM((rows, 4 * units), F32)],
        cost_estimate=cost,
        name="up_last",
    )(x, gu_a, gu_b, start)


def down_kernel(hid_a, hid_b, w0, w1, w2, w3, out_ref):
    weights = jnp.concatenate([w0[...], w1[...], w2[...], w3[...]], axis=0)

    def body(at):
        hidden = jnp.concatenate([hid_a[at, :], hid_b[at, :]], axis=1)
        out_ref[at, :] = jnp.dot(hidden, weights, preferred_element_type=F32).astype(BF16)

    over_tiles(hid_a.shape[0], body)


def down(hid_a, hid_b, pieces):
    rows, units = hid_a.shape
    shard, depth = pieces[0].shape
    hid_spec = pl.BlockSpec((rows, units), lambda i: (0, 0))
    w_spec = pl.BlockSpec((shard, CHUNK), lambda i: (0, i))
    return pl.pallas_call(
        down_kernel,
        grid=(depth // CHUNK,),
        in_specs=[hid_spec, hid_spec] + [w_spec] * 4,
        out_specs=pl.BlockSpec((rows, CHUNK), lambda i: (0, i)),
        out_shape=jax.ShapeDtypeStruct((rows, depth), BF16),
        cost_estimate=pl.CostEstimate(
            flops=2 * rows * depth * units * 2,
            bytes_accessed=2 * rows * depth + 8 * shard * depth + 4 * rows * units,
            transcendentals=0,
        ),
        name="down",
    )(hid_a, hid_b, *pieces)


def put_kernel(moving, got, own, *refs):
    out = refs[-1]

    @pl.when(moving[0] != 0)
    def _():
        out[...] = got[...]

    @pl.when(moving[0] == 0)
    def _():
        out[...] = own[...]


def put(moving, got, own, first, base=None):
    block = 64
    depth = own.shape[1]
    start = first // block
    here = pl.BlockSpec((block, depth), lambda i, m: (start + i, 0))
    specs = [pl.BlockSpec((block, depth), lambda i, m: (i, 0)), here]
    args = [moving, got, own]
    aliases = {}
    if base is not None:
        specs.append(pl.BlockSpec(memory_space=pl.ANY))
        args.append(base)
        aliases = {3: 0}
    return pl.pallas_call(
        put_kernel,
        grid_spec=pltpu.PrefetchScalarGridSpec(
            num_scalar_prefetch=1,
            grid=(got.shape[0] // block,),
            in_specs=specs,
            out_specs=here,
        ),
        out_shape=jax.ShapeDtypeStruct(own.shape, own.dtype),
        input_output_aliases=aliases,
        cost_estimate=pl.CostEstimate(
            flops=0, bytes_accessed=6 * got.shape[0] * depth, transcendentals=0
        ),
        name="put",
    )(*args)


def swap(value, axes):
    count = 2 ** len(axes)
    return lax.ppermute(value, axes, [(i, i ^ (count - 1)) for i in range(count)])


def column(own):
    return jnp.concatenate(
        [own, swap(own, ("h",)), swap(own, ("qh",)), swap(own, ("qh", "h"))], axis=0
    )


def tables(meta, rows, tops, plane, q_high, experts, slots):
    total = meta.shape[0]
    per = slots // experts
    ids = meta[:, :tops]
    e_pos = lax.iota(jnp.int32, experts)
    e_num = (((e_pos >> 1) * 2 + plane) * 2 + (e_pos & 1)).astype(F32)
    hit = ids[:, :, None] == e_num
    named = jnp.any(hit, axis=1)
    g_high = jnp.sum(jnp.where(hit, meta[:, tops : 2 * tops, None], 0.0), axis=1).astype(BF16)
    g_low = jnp.sum(jnp.where(hit, meta[:, 2 * tops : 3 * tops, None], 0.0), axis=1).astype(BF16)
    t_row = lax.broadcasted_iota(jnp.int32, (total, total), 0)
    t_col = lax.broadcasted_iota(jnp.int32, (total, total), 1)
    earlier = ((t_row // rows == t_col // rows) & (t_col < t_row)).astype(BF16)
    rank = jnp.dot(earlier, named.astype(BF16), preferred_element_type=F32)
    place = jnp.where(named, rank, -1.0).astype(BF16)
    spread = (
        lax.broadcasted_iota(jnp.int32, (experts, slots), 0)
        == lax.broadcasted_iota(jnp.int32, (experts, slots), 1) // per
    ).astype(BF16)
    wide = jnp.dot(
        jnp.concatenate([place, g_high, g_low], axis=0), spread, preferred_element_type=F32
    )
    n_col = lax.broadcasted_iota(jnp.int32, (total, slots), 1) % per
    t_blk = lax.broadcasted_iota(jnp.int32, (total, slots), 0) // rows
    t_blk = t_blk ^ (q_high * (total // rows // 2))
    chosen = (n_col // CAP == t_blk) & (wide[:total] == (n_col % CAP).astype(F32))
    mix = jnp.concatenate(
        [
            jnp.where(chosen, wide[total : 2 * total], 0.0),
            jnp.where(chosen, wide[2 * total :], 0.0),
        ],
        axis=0,
    )
    return chosen.astype(BF16), mix.astype(BF16)


def pack(pick, held):
    return lax.dot_general(
        pick, held, (((0,), (0,)), ((), ())), preferred_element_type=F32
    ).astype(BF16)


def across(value, experts):
    slots, depth = value.shape
    return lax.all_to_all(
        value.reshape(experts, slots // experts, depth), PLANE, 0, 0, tiled=True
    ).reshape(slots, depth)


def local(tokens, expert_ids, gate_probs, gate_up, down_proj, pairs):
    steps, rows, depth = tokens.shape
    tops = expert_ids.shape[2]
    half = depth // 2
    plane = lax.axis_index("h")
    q_high = lax.axis_index("qh")
    slot = (
        (lax.axis_index("x") * 4 + lax.axis_index("y")) * 2 + plane
    ) * 2 + lax.axis_index("c")
    own = steps * rows
    experts = 32
    slots = experts * 4 * steps * CAP

    flat = tokens.reshape(own, depth)
    gates = gate_probs.reshape(own, tops)
    high = lax.reduce_precision(gates, 8, 7)
    low = gates - high
    first = jnp.concatenate(
        [
            flat[:, :half],
            expert_ids.reshape(own, tops).astype(BF16),
            high.astype(BF16),
            low.astype(BF16),
            jnp.zeros((own, META - 3 * tops), BF16),
        ],
        axis=1,
    )
    across_x = [(i, i ^ 2) for i in range(4)]
    got_dn = lax.ppermute(down_proj, ("x",), across_x)
    held0 = column(first)
    held1 = column(flat[:, half:])
    gu_b = swap(gate_up, ("ql",))
    mine = lax.dynamic_slice_in_dim(down_proj[0], q_high * half, half, axis=1)
    theirs = lax.dynamic_slice_in_dim(down_proj[0], (1 - q_high) * half, half, axis=1)
    near_piece = swap(mine, ("ql",))
    pieces = [mine, near_piece, swap(theirs, ("qh",)), swap(theirs, ("qh", "ql"))]

    pick, mix = tables(
        held0[:, half:].astype(F32), rows, tops, plane, q_high, experts, slots
    )
    packed0 = pack(pick, held0[:, :half])
    x0 = across(packed0, experts)
    packed1 = pack(pick, held1)
    x1 = across(packed1, experts)
    start = up(x0, gate_up, gu_b, 0)
    hidden = up(x1, gate_up, gu_b, half, start)
    hidden_b = swap(hidden, ("qh",))
    table = gate_up.reshape(-1, depth)
    got_gu0 = lax.ppermute(table[:HEAD], ("x",), across_x)
    got_gu1 = lax.ppermute(table[HEAD:], ("x",), across_x)
    made = down(hidden, hidden_b, pieces)
    back = across(made, experts)
    both = jnp.dot(mix, back, preferred_element_type=F32)
    mixed = both[: 4 * own] + both[4 * own :]
    parts = mixed.reshape(4, own, half)
    sent = parts[1:].astype(BF16)
    near = parts[0] + swap(sent[0], ("h",)).astype(F32)
    far = swap(sent[1], ("qh",)).astype(F32) + swap(sent[2], ("qh", "h")).astype(F32)
    low_half = q_high == 0
    out = jnp.concatenate(
        [jnp.where(low_half, near, far), jnp.where(low_half, far, near)], axis=1
    )
    moving = jnp.any(pairs == slot)
    flag = moving.astype(jnp.int32).reshape(1)
    new_gu = put(flag, got_gu0, table, 0)
    new_gu = put(flag, got_gu1, table, HEAD, new_gu)
    new_dn = jnp.where(moving, got_dn, down_proj)
    return (
        out.astype(BF16).reshape(steps, rows, depth),
        new_gu.reshape(gate_up.shape),
        new_dn,
    )


def solution(mesh):
    fine = Mesh(mesh.devices.reshape(2, 2, 4, 4, 2, 2), ("qh", "ql", "x", "y", "h", "c"))
    dp = ("qh", "ql")
    ex = ("x", "y", "h", "c")
    return jax.shard_map(
        local,
        mesh=fine,
        in_specs=(
            P(None, dp + ex, None),
            P(None, dp + ex, None),
            P(None, dp + ex, None),
            P(ex, None, dp, None),
            P(ex, dp, None),
            P(),
        ),
        out_specs=(
            P(None, dp + ex, None),
            P(ex, None, dp, None),
            P(ex, dp, None),
        ),
        check_vma=False,
    )
```

```python
import jax
import jax.numpy as jnp
from jax import lax
from jax.experimental import pallas as pl
from jax.experimental.pallas import tpu as pltpu
from jax.sharding import Mesh, PartitionSpec as P


F32 = jnp.float32
BF16 = jnp.bfloat16
CAP = 3
CHUNK = 1024
META = 128
HEAD = 288
PLANE = ("x", "y", "c")


def project(x, gu_a, gu_b):
    weights = jnp.concatenate([gu_a[0, 0], gu_b[0, 0], gu_a[0, 1], gu_b[0, 1]], axis=0)
    return lax.dot_general(x[...], weights, (((1,), (1,)), ((), ())), preferred_element_type=F32)


def up_first_kernel(x_ref, gu_a, gu_b, out):
    out[...] = project(x_ref, gu_a, gu_b)


def up_last_kernel(x_ref, gu_a, gu_b, start, hid):
    units = hid.shape[1]
    value = start[...] + project(x_ref, gu_a, gu_b)
    gate = value[:, :units]
    hid[...] = (gate / (1.0 + jnp.exp(-gate)) * value[:, units:]).astype(BF16)


def up(x, gu_a, gu_b, at, start=None):
    rows, depth = x.shape
    units = gu_a.shape[2]
    tile = rows // 2
    gu_spec = pl.BlockSpec((1, 2, units, depth), lambda i: (0, 0, 0, at // depth))
    wide = pl.BlockSpec((tile, 4 * units), lambda i: (i, 0))
    specs = [pl.BlockSpec((tile, depth), lambda i: (i, 0)), gu_spec, gu_spec]
    cost = pl.CostEstimate(
        flops=2 * rows * depth * units * 4,
        bytes_accessed=2 * rows * depth + 8 * units * depth + 16 * rows * units,
        transcendentals=0,
    )
    if start is None:
        return pl.pallas_call(
            up_first_kernel,
            grid=(2,),
            in_specs=specs,
            out_specs=wide,
            out_shape=jax.ShapeDtypeStruct((rows, 4 * units), F32),
            cost_estimate=cost,
            name="up_first",
        )(x, gu_a, gu_b)
    return pl.pallas_call(
        up_last_kernel,
        grid=(2,),
        in_specs=specs + [wide],
        out_specs=pl.BlockSpec((tile, 2 * units), lambda i: (i, 0)),
        out_shape=jax.ShapeDtypeStruct((rows, 2 * units), BF16),
        cost_estimate=cost,
        name="up_last",
    )(x, gu_a, gu_b, start)


def down_kernel(hid_a, hid_b, w0, w1, w2, w3, out_ref):
    hidden = jnp.concatenate([hid_a[...], hid_b[...]], axis=1)
    weights = jnp.concatenate([w0[...], w1[...], w2[...], w3[...]], axis=0)
    out_ref[...] = jnp.dot(hidden, weights, preferred_element_type=F32).astype(BF16)


def down(hid_a, hid_b, pieces):
    rows, units = hid_a.shape
    shard, depth = pieces[0].shape
    hid_spec = pl.BlockSpec((rows, units), lambda i: (0, 0))
    w_spec = pl.BlockSpec((shard, CHUNK), lambda i: (0, i))
    return pl.pallas_call(
        down_kernel,
        grid=(depth // CHUNK,),
        in_specs=[hid_spec, hid_spec] + [w_spec] * 4,
        out_specs=pl.BlockSpec((rows, CHUNK), lambda i: (0, i)),
        out_shape=jax.ShapeDtypeStruct((rows, depth), BF16),
        cost_estimate=pl.CostEstimate(
            flops=2 * rows * depth * units * 2,
            bytes_accessed=2 * rows * depth + 8 * shard * depth + 4 * rows * units,
            transcendentals=0,
        ),
        name="down",
    )(hid_a, hid_b, *pieces)


def put_kernel(moving, got, own, *refs):
    out = refs[-1]

    @pl.when(moving[0] != 0)
    def _():
        out[...] = got[...]

    @pl.when(moving[0] == 0)
    def _():
        out[...] = own[...]


def put(moving, got, own, first, base=None):
    block = 96
    depth = own.shape[1]
    start = first // block
    here = pl.BlockSpec((block, depth), lambda i, m: (start + i, 0))
    specs = [pl.BlockSpec((block, depth), lambda i, m: (i, 0)), here]
    args = [moving, got, own]
    aliases = {}
    if base is not None:
        specs.append(pl.BlockSpec(memory_space=pl.ANY))
        args.append(base)
        aliases = {3: 0}
    return pl.pallas_call(
        put_kernel,
        grid_spec=pltpu.PrefetchScalarGridSpec(
            num_scalar_prefetch=1,
            grid=(got.shape[0] // block,),
            in_specs=specs,
            out_specs=here,
        ),
        out_shape=jax.ShapeDtypeStruct(own.shape, own.dtype),
        input_output_aliases=aliases,
        cost_estimate=pl.CostEstimate(
            flops=0, bytes_accessed=6 * got.shape[0] * depth, transcendentals=0
        ),
        name="put",
    )(*args)


def swap(value, axes):
    count = 2 ** len(axes)
    return lax.ppermute(value, axes, [(i, i ^ (count - 1)) for i in range(count)])


def column(own):
    return jnp.concatenate(
        [own, swap(own, ("h",)), swap(own, ("qh",)), swap(own, ("qh", "h"))], axis=0
    )


def tables(meta, rows, tops, plane, q_high, experts, slots):
    total = meta.shape[0]
    per = slots // experts
    ids = meta[:, :tops]
    e_pos = lax.iota(jnp.int32, experts)
    e_num = (((e_pos >> 1) * 2 + plane) * 2 + (e_pos & 1)).astype(F32)
    hit = ids[:, :, None] == e_num
    named = jnp.any(hit, axis=1)
    g_high = jnp.sum(jnp.where(hit, meta[:, tops : 2 * tops, None], 0.0), axis=1).astype(BF16)
    g_low = jnp.sum(jnp.where(hit, meta[:, 2 * tops : 3 * tops, None], 0.0), axis=1).astype(BF16)
    t_row = lax.broadcasted_iota(jnp.int32, (total, total), 0)
    t_col = lax.broadcasted_iota(jnp.int32, (total, total), 1)
    earlier = ((t_row // rows == t_col // rows) & (t_col < t_row)).astype(BF16)
    rank = jnp.dot(earlier, named.astype(BF16), preferred_element_type=F32)
    place = jnp.where(named, rank, -1.0).astype(BF16)
    spread = (
        lax.broadcasted_iota(jnp.int32, (experts, slots), 0)
        == lax.broadcasted_iota(jnp.int32, (experts, slots), 1) // per
    ).astype(BF16)
    wide = jnp.dot(
        jnp.concatenate([place, g_high, g_low], axis=0), spread, preferred_element_type=F32
    )
    n_col = lax.broadcasted_iota(jnp.int32, (total, slots), 1) % per
    t_blk = lax.broadcasted_iota(jnp.int32, (total, slots), 0) // rows
    t_blk = t_blk ^ (q_high * (total // rows // 2))
    chosen = (n_col // CAP == t_blk) & (wide[:total] == (n_col % CAP).astype(F32))
    mix = jnp.concatenate(
        [
            jnp.where(chosen, wide[total : 2 * total], 0.0),
            jnp.where(chosen, wide[2 * total :], 0.0),
        ],
        axis=0,
    )
    return chosen.astype(BF16), mix.astype(BF16)


def pack(pick, held):
    return lax.dot_general(
        pick, held, (((0,), (0,)), ((), ())), preferred_element_type=F32
    ).astype(BF16)


def across(value, experts):
    slots, depth = value.shape
    return lax.all_to_all(
        value.reshape(experts, slots // experts, depth), PLANE, 0, 0, tiled=True
    ).reshape(slots, depth)


def local(tokens, expert_ids, gate_probs, gate_up, down_proj, pairs):
    steps, rows, depth = tokens.shape
    tops = expert_ids.shape[2]
    half = depth // 2
    late = depth - CHUNK
    plane = lax.axis_index("h")
    q_high = lax.axis_index("qh")
    slot = (
        (lax.axis_index("x") * 4 + lax.axis_index("y")) * 2 + plane
    ) * 2 + lax.axis_index("c")
    own = steps * rows
    experts = 32
    slots = experts * 4 * steps * CAP

    flat = tokens.reshape(own, depth)
    gates = gate_probs.reshape(own, tops)
    high = lax.reduce_precision(gates, 8, 7)
    low = gates - high
    first = jnp.concatenate(
        [
            flat[:, late:],
            expert_ids.reshape(own, tops).astype(BF16),
            high.astype(BF16),
            low.astype(BF16),
            jnp.zeros((own, META - 3 * tops), BF16),
        ],
        axis=1,
    )
    across_x = [(i, i ^ 2) for i in range(4)]
    got_dn = lax.ppermute(down_proj, ("x",), across_x)
    held0 = column(first)
    held1 = column(flat[:, :late])
    gu_b = swap(gate_up, ("ql",))
    mine = lax.dynamic_slice_in_dim(down_proj[0], q_high * half, half, axis=1)
    theirs = lax.dynamic_slice_in_dim(down_proj[0], (1 - q_high) * half, half, axis=1)
    across_piece = swap(theirs, ("qh", "ql"))
    far_piece = swap(theirs, ("qh",))
    near_piece = swap(mine, ("ql",))
    pieces = [mine, near_piece, far_piece, across_piece]

    pick, mix = tables(
        held0[:, CHUNK:].astype(F32), rows, tops, plane, q_high, experts, slots
    )
    packed0 = pack(pick, held0[:, :CHUNK])
    x0 = across(packed0, experts)
    packed1 = pack(pick, held1)
    x1 = across(packed1, experts)
    start = up(x0, gate_up, gu_b, late)
    hidden = up(x1, gate_up, gu_b, 0, start)
    hidden_b = swap(hidden, ("qh",))
    table = gate_up.reshape(-1, depth)
    got_gu0 = lax.ppermute(table[:HEAD], ("x",), across_x)
    got_gu1 = lax.ppermute(table[HEAD:], ("x",), across_x)
    made = down(hidden, hidden_b, pieces)
    back = across(made, experts)
    both = jnp.dot(mix, back, preferred_element_type=F32)
    mixed = both[: 4 * own] + both[4 * own :]
    parts = mixed.reshape(4, own, half)
    sent = parts[1:].astype(BF16)
    near = parts[0] + swap(sent[0], ("h",)).astype(F32)
    far = swap(sent[1], ("qh",)).astype(F32) + swap(sent[2], ("qh", "h")).astype(F32)
    low_half = q_high == 0
    out = jnp.concatenate(
        [jnp.where(low_half, near, far), jnp.where(low_half, far, near)], axis=1
    )
    moving = jnp.any(pairs == slot)
    flag = moving.astype(jnp.int32).reshape(1)
    new_gu = put(flag, got_gu0, table, 0)
    new_gu = put(flag, got_gu1, table, HEAD, new_gu)
    new_dn = jnp.where(moving, got_dn, down_proj)
    return (
        out.astype(BF16).reshape(steps, rows, depth),
        new_gu.reshape(gate_up.shape),
        new_dn,
    )


def solution(mesh):
    fine = Mesh(mesh.devices.reshape(2, 2, 4, 4, 2, 2), ("qh", "ql", "x", "y", "h", "c"))
    dp = ("qh", "ql")
    ex = ("x", "y", "h", "c")
    return jax.shard_map(
        local,
        mesh=fine,
        in_specs=(
            P(None, dp + ex, None),
            P(None, dp + ex, None),
            P(None, dp + ex, None),
            P(ex, None, dp, None),
            P(ex, dp, None),
            P(),
        ),
        out_specs=(
            P(None, dp + ex, None),
            P(ex, None, dp, None),
            P(ex, dp, None),
        ),
        check_vma=False,
    )
```

```python
import jax
import jax.numpy as jnp
from jax import lax
from jax.experimental import pallas as pl
from jax.experimental.pallas import tpu as pltpu
from jax.sharding import Mesh, PartitionSpec as P


F32 = jnp.float32
BF16 = jnp.bfloat16
CAP = 3
CHUNK = 1024
META = 128
HEAD = 336
PLANE = ("x", "y", "c")


def project(x, table):
    return [
        lax.dot_general(x[...], table[0, k], (((1,), (1,)), ((), ())), preferred_element_type=F32)
        for k in range(2)
    ]


def activate(gate, upper):
    return (gate / (1.0 + jnp.exp(-gate)) * upper).astype(BF16)


def own_first_kernel(x, table, gate, upper):
    gate[...], upper[...] = project(x, table)


def own_last_kernel(x, table, gate, upper, hid):
    more = project(x, table)
    hid[...] = activate(gate[...] + more[0], upper[...] + more[1])


def other_kernel(x, x_late, table, table_late, hid):
    one, two = project(x, table), project(x_late, table_late)
    hid[...] = activate(one[0] + two[0], one[1] + two[1])


def row_call(kernel, rows, units, blocks, args, outs):
    tile = rows // 2
    whole = [pl.BlockSpec((tile, units), lambda i: (i, 0)) for _ in outs]
    depth = sum(a.shape[1] for a in args if a.ndim == 2 and a.shape[1] > units)
    return pl.pallas_call(
        kernel,
        grid=(2,),
        in_specs=[
            pl.BlockSpec((1, 2, units, width), lambda i, at=at: (0, 0, 0, at))
            if arg.ndim == 4
            else pl.BlockSpec((tile, arg.shape[1]), lambda i: (i, 0))
            for arg, (width, at) in zip(args, blocks)
        ],
        out_specs=whole,
        out_shape=[jax.ShapeDtypeStruct((rows, units), kind) for kind in outs],
        cost_estimate=pl.CostEstimate(
            flops=4 * rows * depth * units,
            bytes_accessed=2 * rows * depth + 4 * units * depth + 8 * rows * units,
            transcendentals=0,
        ),
    )(*args)


def down_kernel(*refs):
    out_ref = refs[-1]
    hiddens, weights = refs[:4], refs[4:8]
    value = jnp.dot(hiddens[0][...], weights[0][...], preferred_element_type=F32)
    for hidden, weight in zip(hiddens[1:], weights[1:]):
        value += jnp.dot(hidden[...], weight[...], preferred_element_type=F32)
    out_ref[...] = value.astype(BF16)


def down(hiddens, pieces):
    rows, units = hiddens[0].shape
    depth = pieces[0].shape[1]
    width = depth // 4
    hid_spec = pl.BlockSpec(memory_space=pltpu.VMEM)
    w_spec = pl.BlockSpec((units, width), lambda i: (0, i))
    return pl.pallas_call(
        down_kernel,
        grid=(depth // width,),
        in_specs=[hid_spec] * 4 + [w_spec] * 4,
        out_specs=pl.BlockSpec((rows, width), lambda i: (0, i)),
        out_shape=jax.ShapeDtypeStruct((rows, depth), BF16),
        cost_estimate=pl.CostEstimate(
            flops=8 * rows * depth * units,
            bytes_accessed=2 * rows * depth + 8 * units * depth + 8 * rows * units,
            transcendentals=0,
        ),
        name="down",
    )(*hiddens, *pieces)


def put_kernel(moving, got, own, *refs):
    out = refs[-1]

    @pl.when(moving[0] != 0)
    def _():
        out[...] = got[...]

    @pl.when(moving[0] == 0)
    def _():
        out[...] = own[...]


def put(moving, got, own, first, base=None):
    block = 48
    depth = own.shape[1]
    start = first // block
    here = pl.BlockSpec((block, depth), lambda i, m: (start + i, 0))
    specs = [pl.BlockSpec((block, depth), lambda i, m: (i, 0)), here]
    args = [moving, got, own]
    aliases = {}
    if base is not None:
        specs.append(pl.BlockSpec(memory_space=pl.ANY))
        args.append(base)
        aliases = {3: 0}
    return pl.pallas_call(
        put_kernel,
        grid_spec=pltpu.PrefetchScalarGridSpec(
            num_scalar_prefetch=1,
            grid=(got.shape[0] // block,),
            in_specs=specs,
            out_specs=here,
        ),
        out_shape=jax.ShapeDtypeStruct(own.shape, own.dtype),
        input_output_aliases=aliases,
        cost_estimate=pl.CostEstimate(
            flops=0, bytes_accessed=6 * got.shape[0] * depth, transcendentals=0
        ),
        name="put",
    )(*args)


def swap(value, axes):
    count = 2 ** len(axes)
    return lax.ppermute(value, axes, [(i, i ^ (count - 1)) for i in range(count)])


def column(own):
    return jnp.concatenate(
        [own, swap(own, ("h",)), swap(own, ("qh",)), swap(own, ("qh", "h"))], axis=0
    )


def tables(meta, rows, tops, plane, q_high, experts, slots):
    total = meta.shape[0]
    per = slots // experts
    ids = meta[:, :tops]
    e_pos = lax.iota(jnp.int32, experts)
    e_num = (((e_pos >> 1) * 2 + plane) * 2 + (e_pos & 1)).astype(F32)
    hit = ids[:, :, None] == e_num
    named = jnp.any(hit, axis=1)
    g_high = jnp.sum(jnp.where(hit, meta[:, tops : 2 * tops, None], 0.0), axis=1).astype(BF16)
    g_low = jnp.sum(jnp.where(hit, meta[:, 2 * tops : 3 * tops, None], 0.0), axis=1).astype(BF16)
    t_row = lax.broadcasted_iota(jnp.int32, (total, total), 0)
    t_col = lax.broadcasted_iota(jnp.int32, (total, total), 1)
    earlier = ((t_row // rows == t_col // rows) & (t_col < t_row)).astype(BF16)
    rank = jnp.dot(earlier, named.astype(BF16), preferred_element_type=F32)
    place = jnp.where(named, rank, -1.0).astype(BF16)
    spread = (
        lax.broadcasted_iota(jnp.int32, (experts, slots), 0)
        == lax.broadcasted_iota(jnp.int32, (experts, slots), 1) // per
    ).astype(BF16)
    wide = jnp.dot(
        jnp.concatenate([place, g_high, g_low], axis=0), spread, preferred_element_type=F32
    )
    n_col = lax.broadcasted_iota(jnp.int32, (total, slots), 1) % per
    t_blk = lax.broadcasted_iota(jnp.int32, (total, slots), 0) // rows
    t_blk = t_blk ^ (q_high * (total // rows // 2))
    chosen = (n_col // CAP == t_blk) & (wide[:total] == (n_col % CAP).astype(F32))
    mix = jnp.concatenate(
        [
            jnp.where(chosen, wide[total : 2 * total], 0.0),
            jnp.where(chosen, wide[2 * total :], 0.0),
        ],
        axis=0,
    )
    return chosen.astype(BF16), mix.astype(BF16)


def pack(pick, held):
    return lax.dot_general(
        pick, held, (((0,), (0,)), ((), ())), preferred_element_type=F32
    ).astype(BF16)


def across(value, experts):
    slots, depth = value.shape
    return lax.all_to_all(
        value.reshape(experts, slots // experts, depth), PLANE, 0, 0, tiled=True
    ).reshape(slots, depth)


def local(tokens, expert_ids, gate_probs, gate_up, down_proj, pairs):
    steps, rows, depth = tokens.shape
    tops = expert_ids.shape[2]
    half = depth // 2
    late = depth - CHUNK
    plane = lax.axis_index("h")
    q_high = lax.axis_index("qh")
    slot = (
        (lax.axis_index("x") * 4 + lax.axis_index("y")) * 2 + plane
    ) * 2 + lax.axis_index("c")
    own = steps * rows
    experts = 32
    slots = experts * 4 * steps * CAP

    flat = tokens.reshape(own, depth)
    gates = gate_probs.reshape(own, tops)
    high = lax.reduce_precision(gates, 8, 7)
    low = gates - high
    first = jnp.concatenate(
        [
            flat[:, late:],
            expert_ids.reshape(own, tops).astype(BF16),
            high.astype(BF16),
            low.astype(BF16),
            jnp.zeros((own, META - 3 * tops), BF16),
        ],
        axis=1,
    )
    across_x = [(i, i ^ 2) for i in range(4)]
    got_dn = lax.ppermute(down_proj, ("x",), across_x)
    held0 = column(first)
    held1 = column(flat[:, :late])
    gu_b = swap(gate_up, ("ql",))
    mine = lax.dynamic_slice_in_dim(down_proj[0], q_high * half, half, axis=1)
    theirs = lax.dynamic_slice_in_dim(down_proj[0], (1 - q_high) * half, half, axis=1)
    across_piece = swap(theirs, ("qh", "ql"))
    far_piece = swap(theirs, ("qh",))
    near_piece = swap(mine, ("ql",))
    pieces = [mine, near_piece, far_piece, across_piece]

    pick, mix = tables(
        held0[:, CHUNK:].astype(F32), rows, tops, plane, q_high, experts, slots
    )
    packed0 = pack(pick, held0[:, :CHUNK])
    x0 = across(packed0, experts)
    packed1 = pack(pick, held1)
    x1 = across(packed1, experts)
    units = gate_up.shape[2]
    partial = row_call(
        own_first_kernel, slots, units, ((0, 0), (CHUNK, late // CHUNK)), (x0, gate_up), (F32, F32)
    )
    (hidden_a,) = row_call(
        own_last_kernel,
        slots,
        units,
        ((0, 0), (late, 0), (0, 0), (0, 0)),
        (x1, gate_up, *partial),
        (BF16,),
    )
    got_a = swap(hidden_a, ("qh",))
    (hidden_b,) = row_call(
        other_kernel,
        slots,
        units,
        ((0, 0), (0, 0), (CHUNK, late // CHUNK), (late, 0)),
        (x0, x1, gu_b, gu_b),
        (BF16,),
    )
    got_b = swap(hidden_b, ("qh",))
    table = gate_up.reshape(-1, depth)
    got_gu0 = lax.ppermute(table[:HEAD], ("x",), across_x)
    got_gu1 = lax.ppermute(table[HEAD:], ("x",), across_x)
    made = down((hidden_a, hidden_b, got_a, got_b), pieces)
    back = across(made, experts)
    both = jnp.dot(mix, back, preferred_element_type=F32)
    mixed = both[: 4 * own] + both[4 * own :]
    parts = mixed.reshape(4, own, half)
    sent = parts[1:].astype(BF16)
    near = parts[0] + swap(sent[0], ("h",)).astype(F32)
    far = swap(sent[1], ("qh",)).astype(F32) + swap(sent[2], ("qh", "h")).astype(F32)
    low_half = q_high == 0
    out = jnp.concatenate(
        [jnp.where(low_half, near, far), jnp.where(low_half, far, near)], axis=1
    )
    moving = jnp.any(pairs == slot)
    flag = jnp.sum((pairs == slot).astype(jnp.int32)).reshape(1)
    new_gu = put(flag, got_gu0, table, 0)
    new_gu = put(flag, got_gu1, table, HEAD, new_gu)
    new_dn = jnp.where(moving, got_dn, down_proj)
    return (
        out.astype(BF16).reshape(steps, rows, depth),
        new_gu.reshape(gate_up.shape),
        new_dn,
    )


def solution(mesh):
    fine = Mesh(mesh.devices.reshape(2, 2, 4, 4, 2, 2), ("qh", "ql", "x", "y", "h", "c"))
    dp = ("qh", "ql")
    ex = ("x", "y", "h", "c")
    return jax.shard_map(
        local,
        mesh=fine,
        in_specs=(
            P(None, dp + ex, None),
            P(None, dp + ex, None),
            P(None, dp + ex, None),
            P(ex, None, dp, None),
            P(ex, dp, None),
            P(),
        ),
        out_specs=(
            P(None, dp + ex, None),
            P(ex, None, dp, None),
            P(ex, dp, None),
        ),
        check_vma=False,
    )
```

```python
import functools

import jax
import jax.numpy as jnp
from jax import lax
from jax.experimental import pallas as pl
from jax.experimental.pallas import tpu as pltpu
from jax.sharding import Mesh, PartitionSpec as P


F32 = jnp.float32
BF16 = jnp.bfloat16
CAP = 3
CHUNK = 1024
META = 128
HEAD = 336
PLANE = ("x", "y", "c")
CROSS = ("ql", "h")


def project(x, table, at):
    width = x.shape[1]
    return [
        lax.dot_general(
            x[...],
            table[0, k, :, at : at + width],
            (((1,), (1,)), ((), ())),
            preferred_element_type=F32,
        )
        for k in range(2)
    ]


def activate(gate, upper):
    return (gate / (1.0 + jnp.exp(-gate)) * upper).astype(BF16)


def up_kernel(at, x_far, x_late, table, hid, x, sem):
    fetch = pltpu.make_async_copy(x_far, x, sem)
    fetch.start()
    tile = 384
    for m in range(x.shape[0] // tile):
        rows = pl.ds(m * tile, tile)
        two = project(x_late.at[rows], table, 0)
        if m == 0:
            fetch.wait()
        one = project(x.at[rows], table, at)
        hid[rows, :] = activate(one[0] + two[0], one[1] + two[1])


RESIDENT = pl.BlockSpec(memory_space=pltpu.VMEM)
FAR = pl.BlockSpec(memory_space=pltpu.HBM)
ROOM = pltpu.CompilerParams(vmem_limit_bytes=20 * 2**20)


def up(x, x_late, table, at):
    rows, units = x.shape[0], table.shape[2]
    depth = table.shape[3]
    return pl.pallas_call(
        functools.partial(up_kernel, at),
        in_specs=[FAR, RESIDENT, RESIDENT],
        out_specs=RESIDENT,
        out_shape=jax.ShapeDtypeStruct((rows, units), BF16),
        scratch_shapes=[pltpu.VMEM(x.shape, BF16), pltpu.SemaphoreType.DMA],
        compiler_params=ROOM,
        cost_estimate=pl.CostEstimate(
            flops=4 * rows * units * depth,
            bytes_accessed=2 * rows * depth + 4 * units * depth,
            transcendentals=0,
        ),
    )(x, x_late, table)


def down_kernel(*refs):
    hiddens, weights, (out, held, sems) = refs[:4], refs[4:8], refs[8:]
    width = held.shape[2]
    copies = []
    for c in range(held.shape[0]):
        at = pl.ds(c * width, width)
        value = jnp.dot(hiddens[0][...], weights[0][:, at], preferred_element_type=F32)
        for hidden, weight in zip(hiddens[1:], weights[1:]):
            value += jnp.dot(hidden[...], weight[:, at], preferred_element_type=F32)
        held[c] = value.astype(BF16)
        copies.append(pltpu.make_async_copy(held.at[c], out.at[:, at], sems.at[c]))
        copies[-1].start()
    for copy in copies:
        copy.wait()


def down(hiddens, pieces):
    rows, units = hiddens[0].shape
    depth = pieces[0].shape[1]
    parts = 4
    return pl.pallas_call(
        down_kernel,
        in_specs=[RESIDENT] * 8,
        out_specs=FAR,
        out_shape=jax.ShapeDtypeStruct((rows, depth), BF16),
        scratch_shapes=[
            pltpu.VMEM((parts, rows, depth // parts), BF16),
            pltpu.SemaphoreType.DMA((parts,)),
        ],
        compiler_params=ROOM,
        cost_estimate=pl.CostEstimate(
            flops=8 * rows * depth * units,
            bytes_accessed=2 * rows * depth + 8 * units * depth + 8 * rows * units,
            transcendentals=0,
        ),
        name="down",
    )(*hiddens, *pieces)


def put_kernel(moving, got, own, *refs):
    out = refs[-1]

    @pl.when(moving[0] != 0)
    def _():
        out[...] = got[...]

    @pl.when(moving[0] == 0)
    def _():
        out[...] = own[...]


def put(moving, got, own, first, base=None):
    block = 48
    depth = own.shape[1]
    start = first // block
    here = pl.BlockSpec((block, depth), lambda i, m: (start + i, 0))
    specs = [pl.BlockSpec((block, depth), lambda i, m: (i, 0)), here]
    args = [moving, got, own]
    aliases = {}
    if base is not None:
        specs.append(pl.BlockSpec(memory_space=pl.ANY))
        args.append(base)
        aliases = {3: 0}
    return pl.pallas_call(
        put_kernel,
        grid_spec=pltpu.PrefetchScalarGridSpec(
            num_scalar_prefetch=1,
            grid=(got.shape[0] // block,),
            in_specs=specs,
            out_specs=here,
        ),
        out_shape=jax.ShapeDtypeStruct(own.shape, own.dtype),
        input_output_aliases=aliases,
        cost_estimate=pl.CostEstimate(
            flops=0, bytes_accessed=6 * got.shape[0] * depth, transcendentals=0
        ),
        name="put",
    )(*args)


def swap(value, axes):
    count = 2 ** len(axes)
    return lax.ppermute(value, axes, [(i, i ^ (count - 1)) for i in range(count)])


def column(own):
    return jnp.concatenate(
        [own, swap(own, CROSS), swap(own, ("qh",)), swap(own, ("qh",) + CROSS)], axis=0
    )


def tables(meta, rows, tops, plane, q_high, experts, slots):
    total = meta.shape[0]
    per = slots // experts
    ids = meta[:, :tops]
    e_pos = lax.iota(jnp.int32, experts)
    e_num = (((e_pos >> 1) * 2 + plane) * 2 + (e_pos & 1)).astype(F32)
    hit = ids[:, :, None] == e_num
    named = jnp.any(hit, axis=1)
    g_high = jnp.sum(jnp.where(hit, meta[:, tops : 2 * tops, None], 0.0), axis=1).astype(BF16)
    g_low = jnp.sum(jnp.where(hit, meta[:, 2 * tops : 3 * tops, None], 0.0), axis=1).astype(BF16)
    t_row = lax.broadcasted_iota(jnp.int32, (total, total), 0)
    t_col = lax.broadcasted_iota(jnp.int32, (total, total), 1)
    earlier = ((t_row // rows == t_col // rows) & (t_col < t_row)).astype(BF16)
    rank = jnp.dot(earlier, named.astype(BF16), preferred_element_type=F32)
    place = jnp.where(named, rank, -1.0).astype(BF16)
    spread = (
        lax.broadcasted_iota(jnp.int32, (experts, slots), 0)
        == lax.broadcasted_iota(jnp.int32, (experts, slots), 1) // per
    ).astype(BF16)
    wide = jnp.dot(
        jnp.concatenate([place, g_high, g_low], axis=0), spread, preferred_element_type=F32
    )
    n_col = lax.broadcasted_iota(jnp.int32, (total, slots), 1) % per
    t_blk = lax.broadcasted_iota(jnp.int32, (total, slots), 0) // rows
    t_blk = t_blk ^ (q_high * (total // rows // 2))
    chosen = (n_col // CAP == t_blk) & (wide[:total] == (n_col % CAP).astype(F32))
    mix = jnp.concatenate(
        [
            jnp.where(chosen, wide[total : 2 * total], 0.0),
            jnp.where(chosen, wide[2 * total :], 0.0),
        ],
        axis=0,
    )
    return chosen.astype(BF16), mix.astype(BF16)


def pack(pick, held):
    return lax.dot_general(
        pick, held, (((0,), (0,)), ((), ())), preferred_element_type=F32
    ).astype(BF16)


def across(value, experts):
    slots, depth = value.shape
    return lax.all_to_all(
        value.reshape(experts, slots // experts, depth), PLANE, 0, 0, tiled=True
    ).reshape(slots, depth)


def local(tokens, expert_ids, gate_probs, gate_up, down_proj, pairs):
    steps, rows, depth = tokens.shape
    tops = expert_ids.shape[2]
    half = depth // 2
    late = depth - CHUNK
    plane = lax.axis_index("h")
    q_high = lax.axis_index("qh")
    slot = (
        (lax.axis_index("x") * 4 + lax.axis_index("y")) * 2 + plane
    ) * 2 + lax.axis_index("c")
    own = steps * rows
    experts = 32
    slots = experts * 4 * steps * CAP

    flat = tokens.reshape(own, depth)
    gates = gate_probs.reshape(own, tops)
    high = lax.reduce_precision(gates, 8, 7)
    low = gates - high
    first = jnp.concatenate(
        [
            flat[:, late:],
            expert_ids.reshape(own, tops).astype(BF16),
            high.astype(BF16),
            low.astype(BF16),
            jnp.zeros((own, META - 3 * tops), BF16),
        ],
        axis=1,
    )
    across_x = [(i, i ^ 2) for i in range(4)]
    got_dn = lax.ppermute(down_proj, ("x",), across_x)
    held0 = column(first)
    held1 = column(flat[:, :late])
    gu_b = swap(gate_up, ("ql",))
    mine = lax.dynamic_slice_in_dim(down_proj[0], q_high * half, half, axis=1)
    theirs = lax.dynamic_slice_in_dim(down_proj[0], (1 - q_high) * half, half, axis=1)
    across_piece = swap(theirs, ("qh", "ql"))
    far_piece = swap(theirs, ("qh",))
    near_piece = swap(mine, ("ql",))
    pieces = [mine, near_piece, far_piece, across_piece]

    pick, mix = tables(
        held0[:, CHUNK:].astype(F32), rows, tops, plane, q_high, experts, slots
    )
    packed0 = pack(pick, held0[:, :CHUNK])
    x0 = across(packed0, experts)
    packed1 = pack(pick, held1)
    x1 = across(packed1, experts)
    hidden_a = up(x0, x1, gate_up, late)
    got_a = swap(hidden_a, ("qh",))
    hidden_b = up(x0, x1, gu_b, late)
    got_b = swap(hidden_b, ("qh",))
    table = gate_up.reshape(-1, depth)
    got_gu0 = lax.ppermute(table[:HEAD], ("x",), across_x)
    got_gu1 = lax.ppermute(table[HEAD:], ("x",), across_x)
    made = down((hidden_a, hidden_b, got_a, got_b), pieces)
    back = across(made, experts)
    both = jnp.dot(mix, back, preferred_element_type=F32)
    mixed = both[: 4 * own] + both[4 * own :]
    parts = mixed.reshape(4, own, half)
    sent = parts[1:].astype(BF16)
    near = parts[0] + swap(sent[0], CROSS).astype(F32)
    far = swap(sent[1], ("qh",)).astype(F32) + swap(sent[2], ("qh",) + CROSS).astype(F32)
    low_half = q_high == 0
    out = jnp.concatenate(
        [jnp.where(low_half, near, far), jnp.where(low_half, far, near)], axis=1
    )
    moving = jnp.any(pairs == slot)
    flag = jnp.sum((pairs == slot).astype(jnp.int32)).reshape(1)
    new_gu = put(flag, got_gu0, table, 0)
    new_gu = put(flag, got_gu1, table, HEAD, new_gu)
    new_dn = jnp.where(moving, got_dn, down_proj)
    return (
        out.astype(BF16).reshape(steps, rows, depth),
        new_gu.reshape(gate_up.shape),
        new_dn,
    )


def solution(mesh):
    fine = Mesh(mesh.devices.reshape(2, 2, 4, 4, 2, 2), ("qh", "ql", "x", "y", "h", "c"))
    dp = ("qh", "ql")
    ex = ("x", "y", "h", "c")
    return jax.shard_map(
        local,
        mesh=fine,
        in_specs=(
            P(None, dp + ex, None),
            P(None, dp + ex, None),
            P(None, dp + ex, None),
            P(ex, None, dp, None),
            P(ex, dp, None),
            P(),
        ),
        out_specs=(
            P(None, dp + ex, None),
            P(ex, None, dp, None),
            P(ex, dp, None),
        ),
        check_vma=False,
    )
```

```python
import functools

import jax
import jax.numpy as jnp
from jax import lax
from jax.experimental import pallas as pl
from jax.experimental.pallas import tpu as pltpu
from jax.sharding import Mesh, PartitionSpec as P


F32 = jnp.float32
BF16 = jnp.bfloat16
CAP = 3
CHUNK = 1024
META = 128
PLANE = ("x", "y", "c")
CROSS = ("ql", "h")


def project(x, table, at):
    width = x.shape[1]
    return [
        lax.dot_general(
            x[...],
            table[0, k, :, at : at + width],
            (((1,), (1,)), ((), ())),
            preferred_element_type=F32,
        )
        for k in range(2)
    ]


def activate(gate, upper):
    return (gate / (1.0 + jnp.exp(-gate)) * upper).astype(BF16)


def up_kernel(at, x_far, x_late, table, hid, x, sem):
    fetch = pltpu.make_async_copy(x_far, x, sem)
    fetch.start()
    tile = hid.shape[0]
    sides = []
    for m in range(x.shape[0] // tile):
        rows = pl.ds(m * tile, tile)
        two = project(x_late.at[rows], table, 0)
        if m == 0:
            fetch.wait()
        one = project(x.at[rows], table, at)
        sides.append(activate(one[0] + two[0], one[1] + two[1]))
    hid[...] = jnp.concatenate(sides, axis=1)


RESIDENT = pl.BlockSpec(memory_space=pltpu.VMEM)
FAR = pl.BlockSpec(memory_space=pltpu.HBM)
ROOM = pltpu.CompilerParams(vmem_limit_bytes=20 * 2**20)


def up(x, x_late, table, at):
    rows, units = x.shape[0], table.shape[2]
    depth = table.shape[3]
    return pl.pallas_call(
        functools.partial(up_kernel, at),
        in_specs=[FAR, RESIDENT, RESIDENT],
        out_specs=RESIDENT,
        out_shape=jax.ShapeDtypeStruct((rows // 2, 2 * units), BF16),
        scratch_shapes=[pltpu.VMEM(x.shape, BF16), pltpu.SemaphoreType.DMA],
        compiler_params=ROOM,
        cost_estimate=pl.CostEstimate(
            flops=4 * rows * units * depth,
            bytes_accessed=2 * rows * depth + 4 * units * depth,
            transcendentals=0,
        ),
    )(x, x_late, table)


def down_kernel(*refs):
    hiddens, weights, (out, held, sems) = refs[:4], refs[4:8], refs[8:]
    count, rows, width = held.shape
    tile, units = rows // 2, weights[0].shape[0]
    sides = [
        jnp.concatenate([h[:, m * units : (m + 1) * units] for h in hiddens], axis=1)
        for m in range(2)
    ]
    copies = []
    for c in range(count):
        at = pl.ds(c * width, width)
        table = jnp.concatenate([w[:, at] for w in weights], axis=0)
        for m in range(2):
            value = jnp.dot(sides[m], table, preferred_element_type=F32)
            held[c, m * tile : (m + 1) * tile] = value.astype(BF16)
        copies.append(pltpu.make_async_copy(held.at[c], out.at[:, at], sems.at[c]))
        copies[-1].start()
    for copy in copies:
        copy.wait()


def down(hiddens, pieces):
    rows = 2 * hiddens[0].shape[0]
    units, depth = pieces[0].shape
    parts = 4
    return pl.pallas_call(
        down_kernel,
        in_specs=[RESIDENT] * 8,
        out_specs=FAR,
        out_shape=jax.ShapeDtypeStruct((rows, depth), BF16),
        scratch_shapes=[
            pltpu.VMEM((parts, rows, depth // parts), BF16),
            pltpu.SemaphoreType.DMA((parts,)),
        ],
        compiler_params=ROOM,
        cost_estimate=pl.CostEstimate(
            flops=8 * rows * depth * units,
            bytes_accessed=2 * rows * depth + 8 * units * depth + 8 * rows * units,
            transcendentals=0,
        ),
        name="down",
    )(*hiddens, *pieces)


def put_kernel(moving, got, own, out):
    @pl.when(moving[0] != 0)
    def _():
        out[...] = got[...]

    @pl.when(moving[0] == 0)
    def _():
        out[...] = own[...]


def put(moving, got, own):
    block = 64
    depth = own.shape[1]
    spec = pl.BlockSpec((block, depth), lambda i, m: (i, 0))
    return pl.pallas_call(
        put_kernel,
        grid_spec=pltpu.PrefetchScalarGridSpec(
            num_scalar_prefetch=1,
            grid=(got.shape[0] // block,),
            in_specs=[spec, spec],
            out_specs=spec,
        ),
        out_shape=jax.ShapeDtypeStruct(own.shape, own.dtype),
        cost_estimate=pl.CostEstimate(
            flops=0, bytes_accessed=6 * got.shape[0] * depth, transcendentals=0
        ),
        name="put",
    )(moving, got, own)


def swap(value, axes):
    count = 2 ** len(axes)
    return lax.ppermute(value, axes, [(i, i ^ (count - 1)) for i in range(count)])


def column(own):
    return jnp.concatenate(
        [own, swap(own, CROSS), swap(own, ("qh",)), swap(own, ("qh",) + CROSS)], axis=0
    )


def tables(meta, rows, tops, plane, q_high, experts, slots):
    total = meta.shape[0]
    per = slots // experts
    ids = meta[:, :tops]
    e_pos = lax.iota(jnp.int32, experts)
    e_num = (((e_pos >> 1) * 2 + plane) * 2 + (e_pos & 1)).astype(F32)
    hit = ids[:, :, None] == e_num
    named = jnp.any(hit, axis=1)
    g_high = jnp.sum(jnp.where(hit, meta[:, tops : 2 * tops, None], 0.0), axis=1).astype(BF16)
    g_low = jnp.sum(jnp.where(hit, meta[:, 2 * tops : 3 * tops, None], 0.0), axis=1).astype(BF16)
    t_row = lax.broadcasted_iota(jnp.int32, (total, total), 0)
    t_col = lax.broadcasted_iota(jnp.int32, (total, total), 1)
    earlier = ((t_row // rows == t_col // rows) & (t_col < t_row)).astype(BF16)
    rank = jnp.dot(earlier, named.astype(BF16), preferred_element_type=F32)
    place = jnp.where(named, rank, -1.0).astype(BF16)
    spread = (
        lax.broadcasted_iota(jnp.int32, (experts, slots), 0)
        == lax.broadcasted_iota(jnp.int32, (experts, slots), 1) // per
    ).astype(BF16)
    wide = jnp.dot(
        jnp.concatenate([place, g_high, g_low], axis=0), spread, preferred_element_type=F32
    )
    n_col = lax.broadcasted_iota(jnp.int32, (total, slots), 1) % per
    t_blk = lax.broadcasted_iota(jnp.int32, (total, slots), 0) // rows
    t_blk = t_blk ^ (q_high * (total // rows // 2))
    chosen = (n_col // CAP == t_blk) & (wide[:total] == (n_col % CAP).astype(F32))
    mix = jnp.concatenate(
        [
            jnp.where(chosen, wide[total : 2 * total], 0.0),
            jnp.where(chosen, wide[2 * total :], 0.0),
        ],
        axis=0,
    )
    return chosen.astype(BF16), mix.astype(BF16)


def pack(pick, held):
    return lax.dot_general(
        pick, held, (((0,), (0,)), ((), ())), preferred_element_type=F32
    ).astype(BF16)


def across(value, experts):
    slots, depth = value.shape
    return lax.all_to_all(
        value.reshape(experts, slots // experts, depth), PLANE, 0, 0, tiled=True
    ).reshape(slots, depth)


def local(tokens, expert_ids, gate_probs, gate_up, down_proj, pairs):
    steps, rows, depth = tokens.shape
    tops = expert_ids.shape[2]
    half = depth // 2
    late = depth - CHUNK
    plane = lax.axis_index("h")
    q_high = lax.axis_index("qh")
    slot = (
        (lax.axis_index("x") * 4 + lax.axis_index("y")) * 2 + plane
    ) * 2 + lax.axis_index("c")
    own = steps * rows
    experts = 32
    slots = experts * 4 * steps * CAP

    flat = tokens.reshape(own, depth)
    gates = gate_probs.reshape(own, tops)
    high = lax.reduce_precision(gates, 8, 7)
    low = gates - high
    first = jnp.concatenate(
        [
            flat[:, late:],
            expert_ids.reshape(own, tops).astype(BF16),
            high.astype(BF16),
            low.astype(BF16),
            jnp.zeros((own, META - 3 * tops), BF16),
        ],
        axis=1,
    )
    across_x = [(i, i ^ 2) for i in range(4)]
    got_dn = lax.ppermute(down_proj, ("x",), across_x)
    held0 = column(first)
    held1 = column(flat[:, :late])
    gu_b = swap(gate_up, ("ql",))
    mine = lax.dynamic_slice_in_dim(down_proj[0], q_high * half, half, axis=1)
    theirs = lax.dynamic_slice_in_dim(down_proj[0], (1 - q_high) * half, half, axis=1)
    across_piece = swap(theirs, ("qh", "ql"))
    far_piece = swap(theirs, ("qh",))
    near_piece = swap(mine, ("ql",))
    pieces = [mine, near_piece, far_piece, across_piece]

    pick, mix = tables(
        held0[:, CHUNK:].astype(F32), rows, tops, plane, q_high, experts, slots
    )
    packed0 = pack(pick, held0[:, :CHUNK])
    x0 = across(packed0, experts)
    packed1 = pack(pick, held1)
    x1 = across(packed1, experts)
    hidden_a = up(x0, x1, gate_up, late)
    got_a = swap(hidden_a, ("qh",))
    hidden_b = up(x0, x1, gu_b, late)
    got_b = swap(hidden_b, ("qh",))
    table = gate_up.reshape(-1, depth)
    got_gu = lax.ppermute(table, ("x",), across_x)
    made = down((hidden_a, hidden_b, got_a, got_b), pieces)
    back = across(made, experts)
    both = jnp.dot(mix, back, preferred_element_type=F32)
    mixed = both[: 4 * own] + both[4 * own :]
    parts = mixed.reshape(4, own, half)
    sent = parts[1:].astype(BF16)
    near = parts[0] + swap(sent[0], CROSS).astype(F32)
    far = swap(sent[1], ("qh",)).astype(F32) + swap(sent[2], ("qh",) + CROSS).astype(F32)
    low_half = q_high == 0
    out = jnp.concatenate(
        [jnp.where(low_half, near, far), jnp.where(low_half, far, near)], axis=1
    )
    moving = jnp.any(pairs == slot)
    flag = jnp.sum((pairs == slot).astype(jnp.int32)).reshape(1)
    new_gu = put(flag, got_gu, table)
    new_dn = jnp.where(moving, got_dn, down_proj)
    return (
        out.astype(BF16).reshape(steps, rows, depth),
        new_gu.reshape(gate_up.shape),
        new_dn,
    )


def solution(mesh):
    fine = Mesh(mesh.devices.reshape(2, 2, 4, 4, 2, 2), ("qh", "ql", "x", "y", "h", "c"))
    dp = ("qh", "ql")
    ex = ("x", "y", "h", "c")
    return jax.shard_map(
        local,
        mesh=fine,
        in_specs=(
            P(None, dp + ex, None),
            P(None, dp + ex, None),
            P(None, dp + ex, None),
            P(ex, None, dp, None),
            P(ex, dp, None),
            P(),
        ),
        out_specs=(
            P(None, dp + ex, None),
            P(ex, None, dp, None),
            P(ex, dp, None),
        ),
        check_vma=False,
    )
```

```python
import functools

import jax
import jax.numpy as jnp
from jax import lax
from jax.experimental import pallas as pl
from jax.experimental.pallas import tpu as pltpu
from jax.sharding import Mesh, PartitionSpec as P


F32 = jnp.float32
BF16 = jnp.bfloat16
CAP = 3
CHUNK = 1024
META = 128
HEAD = 320
PLANE = ("x", "y", "c")
CROSS = ("ql", "h")


def project(x, table, at):
    width = x.shape[1]
    return [
        lax.dot_general(
            x[...],
            table[0, k, :, at : at + width],
            (((1,), (1,)), ((), ())),
            preferred_element_type=F32,
        )
        for k in range(2)
    ]


def activate(gate, upper):
    return (gate / (1.0 + jnp.exp(-gate)) * upper).astype(BF16)


def up_kernel(at, x_far, x_late, table, hid, x, sem):
    fetch = pltpu.make_async_copy(x_far, x, sem)
    fetch.start()
    tile = hid.shape[0]
    sides = []
    for m in range(x.shape[0] // tile):
        rows = pl.ds(m * tile, tile)
        two = project(x_late.at[rows], table, 0)
        if m == 0:
            fetch.wait()
        one = project(x.at[rows], table, at)
        sides.append(activate(one[0] + two[0], one[1] + two[1]))
    hid[...] = jnp.concatenate(sides, axis=1)


RESIDENT = pl.BlockSpec(memory_space=pltpu.VMEM)
FAR = pl.BlockSpec(memory_space=pltpu.HBM)
ROOM = pltpu.CompilerParams(vmem_limit_bytes=20 * 2**20)


def up(x, x_late, table, at):
    rows, units = x.shape[0], table.shape[2]
    depth = table.shape[3]
    return pl.pallas_call(
        functools.partial(up_kernel, at),
        in_specs=[FAR, RESIDENT, RESIDENT],
        out_specs=RESIDENT,
        out_shape=jax.ShapeDtypeStruct((rows // 2, 2 * units), BF16),
        scratch_shapes=[pltpu.VMEM(x.shape, BF16), pltpu.SemaphoreType.DMA],
        compiler_params=ROOM,
        cost_estimate=pl.CostEstimate(
            flops=4 * rows * units * depth,
            bytes_accessed=2 * rows * depth + 4 * units * depth,
            transcendentals=0,
        ),
    )(x, x_late, table)


def down_kernel(*refs):
    hiddens, weights, (out, held, sems) = refs[:4], refs[4:8], refs[8:]
    count, rows, width = held.shape
    tile, units = rows // 2, weights[0].shape[0]
    sides = [
        jnp.concatenate([h[:, m * units : (m + 1) * units] for h in hiddens], axis=1)
        for m in range(2)
    ]
    copies = []
    for c in range(count):
        at = pl.ds(c * width, width)
        table = jnp.concatenate([w[:, at] for w in weights], axis=0)
        for m in range(2):
            value = jnp.dot(sides[m], table, preferred_element_type=F32)
            held[c, m * tile : (m + 1) * tile] = value.astype(BF16)
        copies.append(pltpu.make_async_copy(held.at[c], out.at[:, at], sems.at[c]))
        copies[-1].start()
    for copy in copies:
        copy.wait()


def down(hiddens, pieces):
    rows = 2 * hiddens[0].shape[0]
    units, depth = pieces[0].shape
    parts = 4
    return pl.pallas_call(
        down_kernel,
        in_specs=[RESIDENT] * 8,
        out_specs=FAR,
        out_shape=jax.ShapeDtypeStruct((rows, depth), BF16),
        scratch_shapes=[
            pltpu.VMEM((parts, rows, depth // parts), BF16),
            pltpu.SemaphoreType.DMA((parts,)),
        ],
        compiler_params=ROOM,
        cost_estimate=pl.CostEstimate(
            flops=8 * rows * depth * units,
            bytes_accessed=2 * rows * depth + 8 * units * depth + 8 * rows * units,
            transcendentals=0,
        ),
        name="down",
    )(*hiddens, *pieces)


def put_kernel(moving, got, own, *refs):
    out = refs[-1]

    @pl.when(moving[0] != 0)
    def _():
        out[...] = got[...]

    @pl.when(moving[0] == 0)
    def _():
        out[...] = own[...]


def put(moving, got, own, first, base=None):
    block = 64
    depth = own.shape[1]
    start = first // block
    here = pl.BlockSpec((block, depth), lambda i, m: (start + i, 0))
    specs = [pl.BlockSpec((block, depth), lambda i, m: (i, 0)), here]
    args = [moving, got, own]
    aliases = {}
    if base is not None:
        specs.append(pl.BlockSpec(memory_space=pl.ANY))
        args.append(base)
        aliases = {3: 0}
    return pl.pallas_call(
        put_kernel,
        grid_spec=pltpu.PrefetchScalarGridSpec(
            num_scalar_prefetch=1,
            grid=(got.shape[0] // block,),
            in_specs=specs,
            out_specs=here,
        ),
        out_shape=jax.ShapeDtypeStruct(own.shape, own.dtype),
        input_output_aliases=aliases,
        cost_estimate=pl.CostEstimate(
            flops=0, bytes_accessed=6 * got.shape[0] * depth, transcendentals=0
        ),
        name="put",
    )(*args)


def swap(value, axes):
    count = 2 ** len(axes)
    return lax.ppermute(value, axes, [(i, i ^ (count - 1)) for i in range(count)])


def column(own):
    return jnp.concatenate(
        [own, swap(own, CROSS), swap(own, ("qh",)), swap(own, ("qh",) + CROSS)], axis=0
    )


def tables(meta, rows, tops, plane, q_high, experts, slots):
    total = meta.shape[0]
    per = slots // experts
    ids = meta[:, :tops]
    e_pos = lax.iota(jnp.int32, experts)
    e_num = (((e_pos >> 1) * 2 + plane) * 2 + (e_pos & 1)).astype(F32)
    hit = ids[:, :, None] == e_num
    named = jnp.any(hit, axis=1)
    g_high = jnp.sum(jnp.where(hit, meta[:, tops : 2 * tops, None], 0.0), axis=1).astype(BF16)
    g_low = jnp.sum(jnp.where(hit, meta[:, 2 * tops : 3 * tops, None], 0.0), axis=1).astype(BF16)
    t_row = lax.broadcasted_iota(jnp.int32, (total, total), 0)
    t_col = lax.broadcasted_iota(jnp.int32, (total, total), 1)
    earlier = ((t_row // rows == t_col // rows) & (t_col < t_row)).astype(BF16)
    rank = jnp.dot(earlier, named.astype(BF16), preferred_element_type=F32)
    place = jnp.where(named, rank, -1.0).astype(BF16)
    spread = (
        lax.broadcasted_iota(jnp.int32, (experts, slots), 0)
        == lax.broadcasted_iota(jnp.int32, (experts, slots), 1) // per
    ).astype(BF16)
    wide = jnp.dot(
        jnp.concatenate([place, g_high, g_low], axis=0), spread, preferred_element_type=F32
    )
    n_col = lax.broadcasted_iota(jnp.int32, (total, slots), 1) % per
    t_blk = lax.broadcasted_iota(jnp.int32, (total, slots), 0) // rows
    t_blk = t_blk ^ (q_high * (total // rows // 2))
    chosen = (n_col // CAP == t_blk) & (wide[:total] == (n_col % CAP).astype(F32))
    mix = jnp.concatenate(
        [
            jnp.where(chosen, wide[total : 2 * total], 0.0),
            jnp.where(chosen, wide[2 * total :], 0.0),
        ],
        axis=0,
    )
    return chosen.astype(BF16), mix.astype(BF16)


def pack(pick, held):
    return lax.dot_general(
        pick, held, (((0,), (0,)), ((), ())), preferred_element_type=F32
    ).astype(BF16)


def across(value, experts):
    slots, depth = value.shape
    return lax.all_to_all(
        value.reshape(experts, slots // experts, depth), PLANE, 0, 0, tiled=True
    ).reshape(slots, depth)


def local(tokens, expert_ids, gate_probs, gate_up, down_proj, pairs):
    steps, rows, depth = tokens.shape
    tops = expert_ids.shape[2]
    half = depth // 2
    late = depth - CHUNK
    plane = lax.axis_index("h")
    q_high = lax.axis_index("qh")
    slot = (
        (lax.axis_index("x") * 4 + lax.axis_index("y")) * 2 + plane
    ) * 2 + lax.axis_index("c")
    own = steps * rows
    experts = 32
    slots = experts * 4 * steps * CAP

    flat = tokens.reshape(own, depth)
    gates = gate_probs.reshape(own, tops)
    high = lax.reduce_precision(gates, 8, 7)
    low = gates - high
    first = jnp.concatenate(
        [
            flat[:, late:],
            expert_ids.reshape(own, tops).astype(BF16),
            high.astype(BF16),
            low.astype(BF16),
            jnp.zeros((own, META - 3 * tops), BF16),
        ],
        axis=1,
    )
    across_x = [(i, i ^ 2) for i in range(4)]
    got_dn = lax.ppermute(down_proj, ("x",), across_x)
    held0 = column(first)
    held1 = column(flat[:, :late])
    gu_b = swap(gate_up, ("ql",))
    mine = lax.dynamic_slice_in_dim(down_proj[0], q_high * half, half, axis=1)
    theirs = lax.dynamic_slice_in_dim(down_proj[0], (1 - q_high) * half, half, axis=1)
    across_piece = swap(theirs, ("qh", "ql"))
    far_piece = swap(theirs, ("qh",))
    near_piece = swap(mine, ("ql",))
    pieces = [mine, near_piece, far_piece, across_piece]

    pick, mix = tables(
        held0[:, CHUNK:].astype(F32), rows, tops, plane, q_high, experts, slots
    )
    packed0 = pack(pick, held0[:, :CHUNK])
    x0 = across(packed0, experts)
    packed1 = pack(pick, held1)
    x1 = across(packed1, experts)
    hidden_a = up(x0, x1, gate_up, late)
    got_a = swap(hidden_a, ("qh",))
    hidden_b = up(x0, x1, gu_b, late)
    got_b = swap(hidden_b, ("qh",))
    table = gate_up.reshape(-1, depth)
    top, rest = table[:HEAD], table[HEAD:]
    got_gu0 = lax.ppermute(top, ("x",), across_x)
    got_gu1 = lax.ppermute(rest, ("x",), across_x)
    made = down((hidden_a, hidden_b, got_a, got_b), pieces)
    back = across(made, experts)
    both = jnp.dot(mix, back, preferred_element_type=F32)
    mixed = both[: 4 * own] + both[4 * own :]
    parts = mixed.reshape(4, own, half)
    sent = parts[1:].astype(BF16)
    near = parts[0] + swap(sent[0], CROSS).astype(F32)
    far = swap(sent[1], ("qh",)).astype(F32) + swap(sent[2], ("qh",) + CROSS).astype(F32)
    low_half = q_high == 0
    out = jnp.concatenate(
        [jnp.where(low_half, near, far), jnp.where(low_half, far, near)], axis=1
    )
    moving = jnp.any(pairs == slot)
    flag = jnp.sum((pairs == slot).astype(jnp.int32)).reshape(1)
    new_gu = put(flag, got_gu0, table, 0)
    new_gu = put(flag, got_gu1, table, HEAD, new_gu)
    new_dn = jnp.where(moving, got_dn, down_proj)
    return (
        out.astype(BF16).reshape(steps, rows, depth),
        new_gu.reshape(gate_up.shape),
        new_dn,
    )


def solution(mesh):
    fine = Mesh(mesh.devices.reshape(2, 2, 4, 4, 2, 2), ("qh", "ql", "x", "y", "h", "c"))
    dp = ("qh", "ql")
    ex = ("x", "y", "h", "c")
    return jax.shard_map(
        local,
        mesh=fine,
        in_specs=(
            P(None, dp + ex, None),
            P(None, dp + ex, None),
            P(None, dp + ex, None),
            P(ex, None, dp, None),
            P(ex, dp, None),
            P(),
        ),
        out_specs=(
            P(None, dp + ex, None),
            P(ex, None, dp, None),
            P(ex, dp, None),
        ),
        check_vma=False,
    )
```

```python
import jax
import jax.numpy as jnp
from jax import lax
from jax.experimental import pallas as pl
from jax.experimental.pallas import tpu as pltpu
from jax.sharding import Mesh, PartitionSpec as P


F32 = jnp.float32
BF16 = jnp.bfloat16
CAP = 3
META = 128
HEAD = 320
PLANE = ("x", "y", "c")
CROSS = ("ql", "h")


def project(x, table):
    return [
        lax.dot_general(x, table[0, k], (((1,), (1,)), ((), ())), preferred_element_type=F32)
        for k in range(2)
    ]


def activate(gate, upper):
    return (gate / (1.0 + jnp.exp(-gate)) * upper).astype(BF16)


def up_kernel(x, table, hid):
    tile = hid.shape[0]
    sides = [
        activate(*project(x[m * tile : (m + 1) * tile], table))
        for m in range(x.shape[0] // tile)
    ]
    hid[...] = jnp.concatenate(sides, axis=1)


RESIDENT = pl.BlockSpec(memory_space=pltpu.VMEM)
FAR = pl.BlockSpec(memory_space=pltpu.HBM)
ROOM = pltpu.CompilerParams(vmem_limit_bytes=20 * 2**20)


def up(x, table):
    rows, units = x.shape[0], table.shape[2]
    depth = table.shape[3]
    return pl.pallas_call(
        up_kernel,
        in_specs=[RESIDENT] * 2,
        out_specs=RESIDENT,
        out_shape=jax.ShapeDtypeStruct((rows // 2, 2 * units), BF16),
        compiler_params=ROOM,
        cost_estimate=pl.CostEstimate(
            flops=4 * rows * units * depth,
            bytes_accessed=2 * rows * depth + 4 * units * depth,
            transcendentals=0,
        ),
    )(x, table)


def down_kernel(*refs):
    hiddens, weights, (out, held, sems) = refs[:4], refs[4:8], refs[8:]
    count, rows, width = held.shape
    tile, units = rows // 2, weights[0].shape[0]
    sides = [
        jnp.concatenate([h[:, m * units : (m + 1) * units] for h in hiddens], axis=1)
        for m in range(2)
    ]
    copies = []
    for c in range(count):
        at = pl.ds(c * width, width)
        table = jnp.concatenate([w[:, at] for w in weights], axis=0)
        for m in range(2):
            value = jnp.dot(sides[m], table, preferred_element_type=F32)
            held[c, m * tile : (m + 1) * tile] = value.astype(BF16)
        copies.append(pltpu.make_async_copy(held.at[c], out.at[:, at], sems.at[c]))
        copies[-1].start()
    for copy in copies:
        copy.wait()


def down(hiddens, pieces):
    rows = 2 * hiddens[0].shape[0]
    units, depth = pieces[0].shape
    parts = 4
    return pl.pallas_call(
        down_kernel,
        in_specs=[RESIDENT] * 8,
        out_specs=FAR,
        out_shape=jax.ShapeDtypeStruct((rows, depth), BF16),
        scratch_shapes=[
            pltpu.VMEM((parts, rows, depth // parts), BF16),
            pltpu.SemaphoreType.DMA((parts,)),
        ],
        compiler_params=ROOM,
        cost_estimate=pl.CostEstimate(
            flops=8 * rows * depth * units,
            bytes_accessed=2 * rows * depth + 8 * units * depth + 8 * rows * units,
            transcendentals=0,
        ),
        name="down",
    )(*hiddens, *pieces)


def put_kernel(moving, got, own, *refs):
    out = refs[-1]

    @pl.when(moving[0] != 0)
    def _():
        out[...] = got[...]

    @pl.when(moving[0] == 0)
    def _():
        out[...] = own[...]


def put(moving, got, own, first, base=None):
    block = 64
    depth = own.shape[1]
    start = first // block
    here = pl.BlockSpec((block, depth), lambda i, m: (start + i, 0))
    specs = [pl.BlockSpec((block, depth), lambda i, m: (i, 0)), here]
    args = [moving, got, own]
    aliases = {}
    if base is not None:
        specs.append(pl.BlockSpec(memory_space=pl.ANY))
        args.append(base)
        aliases = {3: 0}
    return pl.pallas_call(
        put_kernel,
        grid_spec=pltpu.PrefetchScalarGridSpec(
            num_scalar_prefetch=1,
            grid=(got.shape[0] // block,),
            in_specs=specs,
            out_specs=here,
        ),
        out_shape=jax.ShapeDtypeStruct(own.shape, own.dtype),
        input_output_aliases=aliases,
        cost_estimate=pl.CostEstimate(
            flops=0, bytes_accessed=6 * got.shape[0] * depth, transcendentals=0
        ),
        name="put",
    )(*args)


def swap(value, axes):
    count = 2 ** len(axes)
    return lax.ppermute(value, axes, [(i, i ^ (count - 1)) for i in range(count)])


def column(own):
    return jnp.concatenate(
        [own, swap(own, CROSS), swap(own, ("qh",)), swap(own, ("qh",) + CROSS)], axis=0
    )


def tables(meta, rows, tops, plane, q_high, experts, slots):
    total = meta.shape[0]
    per = slots // experts
    ids = meta[:, :tops]
    e_pos = lax.iota(jnp.int32, experts)
    e_num = (((e_pos >> 1) * 2 + plane) * 2 + (e_pos & 1)).astype(F32)
    hit = ids[:, :, None] == e_num
    named = jnp.any(hit, axis=1)
    g_high = jnp.sum(jnp.where(hit, meta[:, tops : 2 * tops, None], 0.0), axis=1).astype(BF16)
    g_low = jnp.sum(jnp.where(hit, meta[:, 2 * tops : 3 * tops, None], 0.0), axis=1).astype(BF16)
    t_row = lax.broadcasted_iota(jnp.int32, (total, total), 0)
    t_col = lax.broadcasted_iota(jnp.int32, (total, total), 1)
    earlier = ((t_row // rows == t_col // rows) & (t_col < t_row)).astype(BF16)
    rank = jnp.dot(earlier, named.astype(BF16), preferred_element_type=F32)
    place = jnp.where(named, rank, -1.0).astype(BF16)
    spread = (
        lax.broadcasted_iota(jnp.int32, (experts, slots), 0)
        == lax.broadcasted_iota(jnp.int32, (experts, slots), 1) // per
    ).astype(BF16)
    wide = jnp.dot(
        jnp.concatenate([place, g_high, g_low], axis=0), spread, preferred_element_type=F32
    )
    n_col = lax.broadcasted_iota(jnp.int32, (total, slots), 1) % per
    t_blk = lax.broadcasted_iota(jnp.int32, (total, slots), 0) // rows
    t_blk = t_blk ^ (q_high * (total // rows // 2))
    chosen = (n_col // CAP == t_blk) & (wide[:total] == (n_col % CAP).astype(F32))
    mix = jnp.concatenate(
        [
            jnp.where(chosen, wide[total : 2 * total], 0.0),
            jnp.where(chosen, wide[2 * total :], 0.0),
        ],
        axis=0,
    )
    return chosen.astype(BF16), mix.astype(BF16)


def pack(pick, held):
    return lax.dot_general(
        pick, held, (((0,), (0,)), ((), ())), preferred_element_type=F32
    ).astype(BF16)


def across(value, experts):
    slots, depth = value.shape
    return lax.all_to_all(
        value.reshape(experts, slots // experts, depth), PLANE, 0, 0, tiled=True
    ).reshape(slots, depth)


def local(tokens, expert_ids, gate_probs, gate_up, down_proj, pairs):
    steps, rows, depth = tokens.shape
    tops = expert_ids.shape[2]
    half = depth // 2
    plane = lax.axis_index("h")
    q_high = lax.axis_index("qh")
    slot = (
        (lax.axis_index("x") * 4 + lax.axis_index("y")) * 2 + plane
    ) * 2 + lax.axis_index("c")
    own = steps * rows
    experts = 32
    slots = experts * 4 * steps * CAP

    flat = tokens.reshape(own, depth)
    gates = gate_probs.reshape(own, tops)
    high = lax.reduce_precision(gates, 8, 7)
    low = gates - high
    first = jnp.concatenate(
        [
            flat,
            expert_ids.reshape(own, tops).astype(BF16),
            high.astype(BF16),
            low.astype(BF16),
            jnp.zeros((own, META - 3 * tops), BF16),
        ],
        axis=1,
    )
    across_x = [(i, i ^ 2) for i in range(4)]
    got_dn = lax.ppermute(down_proj, ("x",), across_x)
    held0 = column(first)
    gu_b = swap(gate_up, ("ql",))
    mine = lax.dynamic_slice_in_dim(down_proj[0], q_high * half, half, axis=1)
    theirs = lax.dynamic_slice_in_dim(down_proj[0], (1 - q_high) * half, half, axis=1)
    across_piece = swap(theirs, ("qh", "ql"))
    far_piece = swap(theirs, ("qh",))
    near_piece = swap(mine, ("ql",))
    pieces = [mine, near_piece, far_piece, across_piece]

    pick, mix = tables(
        held0[:, depth:].astype(F32), rows, tops, plane, q_high, experts, slots
    )
    packed0 = pack(pick, held0[:, :depth])
    x0 = across(packed0, experts)
    hidden_a = up(x0, gate_up)
    got_a = swap(hidden_a, ("qh",))
    hidden_b = up(x0, gu_b)
    got_b = swap(hidden_b, ("qh",))
    table = gate_up.reshape(-1, depth)
    top, rest = table[:HEAD], table[HEAD:]
    got_gu0 = lax.ppermute(top, ("x",), across_x)
    got_gu1 = lax.ppermute(rest, ("x",), across_x)
    made = down((hidden_a, hidden_b, got_a, got_b), pieces)
    back = across(made, experts)
    both = jnp.dot(mix, back, preferred_element_type=F32)
    mixed = both[: 4 * own] + both[4 * own :]
    parts = mixed.reshape(4, own, half)
    sent = parts[1:].astype(BF16)
    near = parts[0] + swap(sent[0], CROSS).astype(F32)
    far = swap(sent[1], ("qh",)).astype(F32) + swap(sent[2], ("qh",) + CROSS).astype(F32)
    low_half = q_high == 0
    out = jnp.concatenate(
        [jnp.where(low_half, near, far), jnp.where(low_half, far, near)], axis=1
    )
    moving = jnp.any(pairs == slot)
    flag = jnp.sum((pairs == slot).astype(jnp.int32)).reshape(1)
    new_gu = put(flag, got_gu0, table, 0)
    new_gu = put(flag, got_gu1, table, HEAD, new_gu)
    new_dn = jnp.where(moving, got_dn, down_proj)
    return (
        out.astype(BF16).reshape(steps, rows, depth),
        new_gu.reshape(gate_up.shape),
        new_dn,
    )


def solution(mesh):
    fine = Mesh(mesh.devices.reshape(2, 2, 4, 4, 2, 2), ("qh", "ql", "x", "y", "h", "c"))
    dp = ("qh", "ql")
    ex = ("x", "y", "h", "c")
    return jax.shard_map(
        local,
        mesh=fine,
        in_specs=(
            P(None, dp + ex, None),
            P(None, dp + ex, None),
            P(None, dp + ex, None),
            P(ex, None, dp, None),
            P(ex, dp, None),
            P(),
        ),
        out_specs=(
            P(None, dp + ex, None),
            P(ex, None, dp, None),
            P(ex, dp, None),
        ),
        check_vma=False,
    )
```
